512 devices in a mesh: dp: 16 (over x, y_hi, core), expert: 32 (over y_lo, z).
Axes of the slice: x: 4, y: 4 (y_hi: 2, y_lo: 2; y = y_hi * 2 + y_lo), z: 16, core: 2. Of those that a mesh axis runs over, the one named last changes fastest.
Arguments:
- hidden_in: bfloat16 [32, 1024, 2048], P('expert', 'dp'), may hold values from -6 to 6
- queries: bfloat16 [32, 1024, 2048], P('expert', None, 'dp'), may hold values from -150 to 150
- key_pool: bfloat16 [256, 128, 2048], P('expert', None, 'dp'), may hold values from -8 to 8
- value_pool: bfloat16 [256, 128, 2048], P('expert', None, 'dp'), may hold values from -6 to 6
- page_table: int32 [32, 8], P('expert'), may hold values from 0 to 7, as said below
- prompt_lengths: int32 [32, 4], P('expert'), may hold values from 1 to 512, 1024 in all within a row
- expert_ids: int32 [32, 1024, 8], P('expert', 'dp'), may hold values from 0 to 31, all different within a row; in each aligned block of 64 rows (0 to 63, 64 to 127, ..., all dimensions but the last counted through in order) at most 20 rows name the same one
- gate_weights: float32 [32, 1024, 8], P('expert', 'dp'), may hold values from 0.05 to 0.3
- norm_gain: float32 [2048], replicated, may hold values from 0.5 to 1.5
- trainer_gate_up: float32 [32, 2048, 2048], P('expert', 'dp'), may hold values from -0.125 to 0.125
- trainer_down: float32 [32, 1024, 2048], P('expert', 'dp'), may hold values from -0.1875 to 0.1875
Outputs:
- mixed: bfloat16 [32, 1024, 2048], P('expert', 'dp')
The draws below stay inside these ranges and needn't reach their ends.
Inputs may be any that keep to these rules, and one draw needn't show every extreme that they name: `page_table`: each group's row is a permutation of the group's page numbers. `expert_ids`: among the 64 rows of one device (aligned blocks of rows), no expert is named by more than 20 rows, a bound that some block reaches.
All inputs are finite; a program needn't handle non-finite values.
Results may differ from the reference program's by a relative error of at most 0.0075.
Values may be sent and summed in bfloat16 or wider, within the bound.
A program may use at most 64 MiB of HBM per device.

```python
import math
import jax
import jax.numpy as jnp
import numpy as np
from jax import lax

D = 2048
HEADS = 16
HDIM = 128
FF = 1024
TOPK = 8
PAGE = 128
REQS = 4
T_DEV = 64
EXPERTS = 32
GROUPS = 32
COL_TOK = 1024
PAGES_COL = 8
MAXLEN = 512
CAP = 20
N_DP = 16


def shared_draw(key):
    perm_keys = jax.random.split(jax.random.fold_in(key, 101), GROUPS)
    permutations = jax.vmap(lambda sub_key: jax.random.permutation(sub_key, PAGES_COL))(perm_keys).astype(jnp.int32)
    logical = jax.random.normal(jax.random.fold_in(key, 102), (GROUPS, COL_TOK // 2, 2, D), jnp.float32)
    logical = jnp.clip(logical.reshape(GROUPS, COL_TOK, D), -6.0, 6.0)
    return (permutations, logical)


def draw_page_table(key, part):
    permutations, logical = shared_draw(key)
    return permutations


def draw_key_pool(key, part):
    permutations, logical = shared_draw(key)
    page_rows = logical.reshape(GROUPS, PAGES_COL, PAGE, D)
    group_index = jnp.arange(GROUPS, dtype=jnp.int32)[:, None]
    physical = jnp.zeros_like(page_rows).at[group_index, permutations].set(page_rows)
    return physical.reshape(GROUPS * PAGES_COL, PAGE, D).astype(jnp.bfloat16)


def draw_queries(key, part):
    drawn = jnp.clip(jax.random.normal(jax.random.fold_in(key, 104), (GROUPS, COL_TOK, D), jnp.float32), -6.0, 6.0)
    return drawn.astype(jnp.bfloat16)


def level_of(key, dims, cuts, smallest, largest):
    factor_of, own = 1.0, jax.random.fold_in(key, 6)
    for axis_at, parts in cuts:
        heights = jnp.exp(jax.random.uniform(jax.random.fold_in(own, axis_at), (parts,), jnp.float32, smallest / len(cuts), largest / len(cuts)))
        factor_of = factor_of * jnp.repeat(heights, dims[axis_at] // parts).reshape([-1 if axis == axis_at else 1 for axis in range(len(dims))])
    return factor_of


def profile(count, total, most, skew):
    weights = [(1 << 20) // math.isqrt(grade ** skew) + 1 for grade in range(2, count + 1)]
    spare, given = total - most - (count - 1), [1] * (count - 1)
    while spare > 0:
        free = [i for i in range(count - 1) if given[i] < most]
        mass, left = sum([weights[i] for i in free]), spare
        for i in free:
            addition = min(most - given[i], max(1, left * weights[i] // mass), spare)
            given[i] = given[i] + addition
            spare = spare - addition
    return np.array([most] + given)


def uneven(key, count, total, limit, lean):
    if count == 2:
        one = jax.random.randint(key, (), max(1, total - limit), min(limit, total - 1) + 1)
        return jnp.stack([one, total - one])
    sizes = jnp.asarray(profile(count, total, limit, lean), jnp.int32)
    pairs = (count - 1) // 2
    giver, taker = sizes[1:1 + 2 * pairs:2], sizes[2:2 + 2 * pairs:2]
    room = jnp.minimum(giver - 1, limit - taker)
    shifted = jax.random.randint(jax.random.fold_in(key, 1), (pairs,), 0, 1 << 20) % (room + 1)
    sizes = sizes.at[1:1 + 2 * pairs:2].set(giver - shifted).at[2:2 + 2 * pairs:2].set(taker + shifted)
    return sizes[jax.random.permutation(jax.random.fold_in(key, 2), count)]


def routed_block(own_key, own, number, rows, count, top, most, skew):
    sequence = jax.random.permutation(own_key, count)
    packed, usual = load_shares(count, rows * top, most, skew, True), load_shares(count, rows * top, most, skew, False)
    places = jnp.arange(count)

    def named(tallies, turn):
        used = int((tallies > 0).sum())
        fixed = max(1, used // 4)
        passed = fixed + (places - fixed + turn * (used - fixed)) % max(1, count - fixed)
        return jnp.zeros((count,), jnp.int32).at[sequence[jnp.where(places < fixed, places, passed)]].set(jnp.asarray(tallies, jnp.int32))

    tallies = jnp.where(number % 4 == 0, named(packed, number // 4), named(usual, number - number // 4 - 1))
    mixed = jax.random.permutation(jax.random.fold_in(own, 3), count)
    donor, receiver = mixed[0:count // 2 * 2:2], mixed[1:count // 2 * 2:2]
    slack = jnp.minimum(tallies[donor] - 1, most - tallies[receiver]) // 2
    slack = jnp.where((donor == sequence[0]) | (receiver == sequence[0]) | (tallies[receiver] == 0), 0, jnp.maximum(slack, 0))
    passed = jax.random.randint(jax.random.fold_in(own, 4), (count // 2,), 0, 1 << 20) % (slack + 1)
    tallies = tallies.at[donor].add(-passed).at[receiver].add(passed)
    items = jnp.searchsorted(jnp.cumsum(tallies), jnp.arange(rows * top), side="right").astype(jnp.int32)
    listing = items.reshape(top, rows).T
    listing = listing[jax.random.permutation(jax.random.fold_in(own, 1), rows)]
    turn = jax.random.randint(jax.random.fold_in(own, 2), (rows, 1), 0, top)
    return jnp.take_along_axis(listing, (jnp.arange(top)[None, :] + turn) % top, axis=1)


def load_shares(number_of, total, reach, lean, full):
    weights = [(1 << 20) // math.isqrt(rank ** lean) + 1 for rank in range(1, number_of + 1)]
    largest = reach if full else min(reach, max(-(-total // number_of), total * weights[0] // sum(weights)))
    least = 1 if total - largest >= number_of - 1 else 0
    given, spare = [largest] + [least] * (number_of - 1), total - largest - least * (number_of - 1)
    while spare > 0:
        free = [i for i in range(1, number_of) if given[i] < largest] or [i for i in range(1, number_of) if given[i] < reach]
        pool, budget = sum([weights[i] for i in free]), spare
        for i in free:
            extra = min(reach - given[i], max(1, budget * weights[i] // pool), spare)
            given[i] = given[i] + extra
            spare = spare - extra
    return np.array(given)


def gaussian(own_key, extent, deviation, most, shards=(), held_as=jnp.bfloat16):
    entries = jax.random.normal(own_key, extent, jnp.float32) * deviation
    if len(shards) > 0:
        entries = level_of(own_key, extent, shards, -0.22, 0.18) * entries
    return jnp.clip(entries, min=-most, max=most).astype(held_as)


def setup_inputs(seed: int = 0) -> dict:
    keys = jax.random.split(jax.random.key(seed), 12)
    hidden_in = gaussian(keys[0], (GROUPS, COL_TOK, D), 1.0, 6.0, ((0, 32), (1, 16)))
    queries = draw_queries(jax.random.fold_in(keys[11], 71), 0)
    key_pool = draw_key_pool(jax.random.fold_in(keys[11], 71), 0)
    value_pool = gaussian(keys[3], (GROUPS * PAGES_COL, PAGE, D), 1.0, 6.0, ((0, 32), (2, 16)))
    page_table = draw_page_table(jax.random.fold_in(keys[11], 71), 0)
    prompt_lengths = jax.vmap(lambda own: uneven(own, REQS, COL_TOK, MAXLEN, 2))(jax.random.split(keys[5], GROUPS)).reshape((GROUPS, REQS)).astype(jnp.int32)
    expert_ids_keys = jax.random.split(jax.random.fold_in(keys[6], 1), GROUPS * COL_TOK // T_DEV)
    expert_ids_turns = jax.random.permutation(jax.random.fold_in(keys[6], 3), GROUPS * COL_TOK // T_DEV)
    expert_ids = jax.vmap(lambda own, number: routed_block(jax.random.fold_in(keys[6], 2), own, number, T_DEV, EXPERTS, TOPK, CAP, 2))(expert_ids_keys, expert_ids_turns).reshape((GROUPS, COL_TOK, TOPK))
    gate_weights = jnp.clip(0.05 + 0.25 * jax.random.uniform(keys[7], (GROUPS, COL_TOK, TOPK), jnp.float32) ** level_of(keys[7], (GROUPS, COL_TOK, TOPK), ((0, 32), (1, 16)), -0.2, 0.2), 0.05, 0.3)
    norm_gain = jnp.clip(1.0 + 0.1 * jax.random.normal(keys[8], (D,), jnp.float32), 0.5, 1.5)
    trainer_gate_up = gaussian(keys[9], (EXPERTS, D, 2 * FF), D ** -0.5, 0.125, ((0, 32), (1, 16)), jnp.float32)
    trainer_down = gaussian(keys[10], (EXPERTS, FF, D), FF ** -0.5, 0.1875, ((0, 32), (1, 16)), jnp.float32)
    return dict(hidden_in=hidden_in, queries=queries, key_pool=key_pool, value_pool=value_pool, page_table=page_table, prompt_lengths=prompt_lengths, expert_ids=expert_ids, gate_weights=gate_weights, norm_gain=norm_gain, trainer_gate_up=trainer_gate_up, trainer_down=trainer_down)


epsilon = 1e-05

def group_attention(operands):
    group_queries, key_pages, value_pages, table_row, length_row = operands
    keys_all = jnp.take(key_pages, table_row, axis=0).reshape(COL_TOK, HEADS, HDIM).astype(jnp.float32)
    values_all = jnp.take(value_pages, table_row, axis=0).reshape(COL_TOK, HEADS, HDIM).astype(jnp.float32)
    request_ends = jnp.cumsum(length_row).astype(jnp.int32)
    positions = jnp.arange(COL_TOK, dtype=jnp.int32)
    request = lax.optimization_barrier(jnp.sum((positions[:, None] >= request_ends[None, :]).astype(jnp.int32), axis=1))
    block_rows = math.gcd(COL_TOK, 512)
    query_blocks = group_queries.reshape(COL_TOK // block_rows, block_rows, HEADS, HDIM)
    request_blocks = request.reshape(COL_TOK // block_rows, block_rows)
    score_scale = 1.0 / math.sqrt(HDIM)

    def attend(pieces):
        query_block, request_block = pieces
        scores = jnp.einsum('qhd,khd->hqk', query_block.astype(jnp.float32), keys_all) * score_scale
        same_request = (request_block[:, None] == request[None, :])[None]
        scores = jnp.where(same_request, scores, -1e+30)
        highest = lax.optimization_barrier(jnp.max(scores, axis=-1, keepdims=True))
        weights = jnp.where(same_request, jnp.exp(scores - highest), 0.0)
        totals = lax.optimization_barrier(jnp.sum(weights, axis=-1, keepdims=True))
        probs = (weights / totals).astype(jnp.bfloat16)
        output = jnp.einsum('hqk,khd->qhd', probs.astype(jnp.float32), values_all)
        return output.astype(jnp.bfloat16).reshape(block_rows, HEADS * HDIM)
    return lax.map(attend, (query_blocks, request_blocks)).reshape(COL_TOK, HEADS * HDIM)

def reference(hidden_in, queries, key_pool, value_pool, page_table, prompt_lengths, expert_ids, gate_weights, norm_gain, trainer_gate_up, trainer_down):
    server_gate_up = trainer_gate_up.astype(jnp.bfloat16)
    server_down = trainer_down.astype(jnp.bfloat16)
    key_pages = key_pool.reshape(GROUPS, PAGES_COL, PAGE, D)
    value_pages = value_pool.reshape(GROUPS, PAGES_COL, PAGE, D)
    attn = lax.map(group_attention, (queries, key_pages, value_pages, page_table, prompt_lengths))
    resid = (hidden_in.astype(jnp.float32) + attn.astype(jnp.float32)).astype(jnp.bfloat16)
    resid32 = resid.astype(jnp.float32)
    mean_square = lax.optimization_barrier(jnp.mean(resid32 * resid32, axis=-1, keepdims=True))
    normed = (resid32 * lax.rsqrt(mean_square + epsilon) * norm_gain).astype(jnp.bfloat16)
    token_count = GROUPS * COL_TOK
    normed_flat = normed.reshape(token_count, D)
    ids_flat = expert_ids.reshape(token_count * TOPK).astype(jnp.int32)
    weights_flat = gate_weights.reshape(token_count * TOPK)
    order = jnp.argsort(ids_flat, stable=True).astype(jnp.int32)
    counts = lax.optimization_barrier(jnp.sum((ids_flat[:, None] == jnp.arange(EXPERTS, dtype=jnp.int32)[None, :]).astype(jnp.int32), axis=0))
    starts = (jnp.cumsum(counts) - counts).astype(jnp.int32)
    bound = CAP * GROUPS * N_DP
    padded_order = jnp.concatenate([order, jnp.zeros((bound,), jnp.int32)])

    def per_expert(running, expert):
        copy_index = lax.dynamic_slice_in_dim(padded_order, starts[expert], bound)
        valid = jnp.arange(bound, dtype=jnp.int32) < counts[expert]
        token_index = (copy_index // TOPK).astype(jnp.int32)
        slot_rows = jnp.take(normed_flat, token_index, axis=0)
        gate_up = jnp.dot(slot_rows, server_gate_up[expert], preferred_element_type=jnp.float32)
        hidden_units = (jax.nn.silu(gate_up[:, :FF]) * gate_up[:, FF:]).astype(jnp.bfloat16)
        outputs = jnp.dot(hidden_units, server_down[expert], preferred_element_type=jnp.float32).astype(jnp.bfloat16)
        weight_col = jnp.where(valid, jnp.take(weights_flat, copy_index), 0.0)
        running = running.at[token_index].add(outputs.astype(jnp.float32) * weight_col[:, None])
        return (running, None)
    mixture, unused = lax.scan(per_expert, jnp.zeros((token_count, D), jnp.float32), jnp.arange(EXPERTS, dtype=jnp.int32))
    mixed = resid32.reshape(token_count, D) + mixture
    return mixed.astype(jnp.bfloat16).reshape(GROUPS, COL_TOK, D)
```

```python
import math

import jax
import jax.numpy as jnp
from jax import lax
from jax.experimental import pallas as pl
from jax.experimental.pallas import tpu as pltpu
from jax.sharding import PartitionSpec as P

MESH = pl.DeviceIdType.MESH
HDIM = 128
TOPK = 8
D = 2048
FF = 1024
NZ = 16
TOK = 64
SUB = TOK // 2
CAP = 20
GRP = 4
GSLOT = GRP * CAP
GTOK = GRP * TOK
NGRP = NZ // GRP
COL = 1024
PAGE = 128
PAGES = COL // PAGE
REQS = 4
QROWS = 256
epsilon = 1e-05

ORDER = (8, 7, 9, 6, 10, 5, 11, 4, 12, 3, 13, 2, 14, 1, 15, 0)
POS = {s: i for i, s in enumerate(ORDER)}

ROWS = (128, 64)
KS = (0, 1, -1, 2)
NMSG = 4 + 4 * len(KS)


def moe_kernel(
    hidden_ref,
    attn_ref,
    gain_ref,
    ids_ref,
    gates_ref,
    gu_hbm,
    dn_hbm,
    out_ref,
    x_buf,
    wg,
    wd,
    gu32,
    dn32,
    xs,
    act,
    outw,
    wcol,
    st,
    ctr,
    rsr,
    rsl,
    resid_s,
    load_sem,
    wsend,
    wrecv,
    sibsend,
    sibrecv,
    agsend,
    agrecv,
    rssend,
    rsrecv,
):
    dp = lax.axis_index("dp")
    ex = lax.axis_index("expert")
    x = dp // 4
    y = ((dp // 2) % 2) * 2 + ex // NZ
    core = dp % 2
    z = ex % NZ

    def dev(xx, yy, zz, cc):
        return ((xx * 2 + yy // 2) * 2 + cc, (yy % 2) * NZ + zz)

    def ring4(v, k):
        return (v + 4 + k) % 4

    sibling = dev(x, y, z, 1 - core)
    zr = dev(x, y, (z + 1) % NZ, core)
    zl = dev(x, y, (z + NZ - 1) % NZ, core)
    xy = {
        (0, 1): dev(ring4(x, 1), y, z, core),
        (0, -1): dev(ring4(x, -1), y, z, core),
        (1, 1): dev(x, ring4(y, 1), z, core),
        (1, -1): dev(x, ring4(y, -1), z, core),
    }

    load_gu = pltpu.make_async_copy(gu_hbm, gu32, load_sem.at[0])
    load_dn = pltpu.make_async_copy(dn_hbm, dn32, load_sem.at[1])
    load_gu.start()
    load_dn.start()

    barrier = pltpu.get_barrier_semaphore()
    partners = [sibling, zr, zl] + list(xy.values())
    for partner in partners:
        pl.semaphore_signal(barrier, inc=1, device_id=partner, device_id_type=MESH)

    pending = []

    def send(src, dst, ssem, rsem, to):
        copy = pltpu.make_async_remote_copy(
            src_ref=src,
            dst_ref=dst,
            send_sem=ssem,
            recv_sem=rsem,
            device_id=to,
            device_id_type=MESH,
        )
        copy.start()
        pending.append(copy)
        return copy

    def arrived(ref, ssem, rsem, to):
        pltpu.make_async_remote_copy(
            src_ref=ref,
            dst_ref=ref,
            send_sem=ssem,
            recv_sem=rsem,
            device_id=to,
            device_id_type=MESH,
        ).wait_recv()

    def shard(stream, dx, dy, off, n):
        sx, sy = ring4(x, -dx), ring4(y, -dy)
        rows = ROWS[stream]
        first = pl.multiple_of(((sx * 2 + sy // 2) * 2 + core) * rows + off, 16)
        buf = wd if stream else wg
        return buf.at[sy % 2, pl.ds(first, n), :]

    def piece(stream, half, k1, k2, part):
        h = ROWS[stream] // 2
        q = h // 2
        off, n = (half * h, h) if part is None else (half * h + part * q, q)
        dx, dy = (k1, k2) if half == 0 else (k2, k1)
        return shard(stream, dx, dy, off, n)

    def wmsg(stream, half, index):
        at = (stream * 2 + half) * NMSG + index
        return wsend.at[at], wrecv.at[at]

    def decode(index):
        if index < 4:
            return 0, (1, -1)[index % 2], index >= 2, 0
        return 1, (1, -1)[index % 2], (index - 4) % 4 >= 2, KS[(index - 4) // 4]

    def wstart(stream, index):
        ring, sign, forward, k = decode(index)
        for half in (0, 1):
            axis = ring if half == 0 else 1 - ring
            part = (0 if sign == 1 else 1) if forward else None
            step = sign if forward else 0
            k1, k2 = (step, 0) if ring == 0 else (k, step)
            ref = piece(stream, half, k1, k2, part)
            ssem, rsem = wmsg(stream, half, index)
            send(ref, ref, ssem, rsem, xy[axis, sign])

    def wwait(stream, index):
        ring, sign, forward, k = decode(index)
        for half in (0, 1):
            axis = ring if half == 0 else 1 - ring
            part = (0 if sign == 1 else 1) if forward else None
            step = 2 if forward else sign
            k1, k2 = (step, 0) if ring == 0 else (k, step)
            ref = piece(stream, half, k1, k2, part)
            ssem, rsem = wmsg(stream, half, index)
            arrived(ref, ssem, rsem, xy[axis, sign])

    def p2(k, j):
        return 4 + 4 * KS.index(k) + j

    sib_index = {}

    def sib(stream, places):
        for dx, dy in places:
            at = stream * 16 + (dx % 4) * 4 + (dy % 4)
            ref = shard(stream, dx, dy, 0, ROWS[stream])
            send(ref, ref, sibsend.at[at], sibrecv.at[at], sibling)
            sib_index[at] = (stream, dx, dy)

    def sib_wait(stream):
        for at, (s, dx, dy) in sib_index.items():
            if s == stream:
                sx, sy = ring4(x, -dx), ring4(y, -dy)
                rows = ROWS[stream]
                first = pl.multiple_of(((sx * 2 + sy // 2) * 2 + 1 - core) * rows, 16)
                buf = wd if stream else wg
                ref = buf.at[sy % 2, pl.ds(first, rows), :]
                arrived(ref, sibsend.at[at], sibrecv.at[at], sibling)

    def weights(stream, phase):
        if phase == 0:
            (load_gu, load_dn)[stream].wait()
            src = (gu32, dn32)[stream]
            rows = ROWS[stream]
            first = pl.multiple_of(dp * rows, 16)
            (wg, wd)[stream][y % 2, pl.ds(first, rows), :] = src[...].astype(jnp.bfloat16)
            if stream == 0:
                pl.semaphore_wait(barrier, len(partners))
            for index in (0, 1, p2(0, 0), p2(0, 1)):
                wstart(stream, index)
            sib(stream, [(0, 0)])
        elif phase == 1:
            for index in (0, 1):
                wwait(stream, index)
            for index in (2, 3, p2(1, 0), p2(1, 1), p2(-1, 0), p2(-1, 1)):
                wstart(stream, index)
        elif phase == 2:
            for index in (p2(0, 0), p2(0, 1)):
                wwait(stream, index)
            for index in (p2(0, 2), p2(0, 3)):
                wstart(stream, index)
            sib(stream, [(1, 0), (-1, 0), (0, 1), (0, -1)])
        elif phase == 3:
            for index in (2, 3):
                wwait(stream, index)
            for index in (p2(2, 0), p2(2, 1)):
                wstart(stream, index)
        elif phase == 4:
            for index in (p2(1, 0), p2(1, 1), p2(-1, 0), p2(-1, 1)):
                wwait(stream, index)
            for index in (p2(1, 2), p2(1, 3), p2(-1, 2), p2(-1, 3)):
                wstart(stream, index)
            sib(stream, [(1, 1), (-1, 1), (1, -1), (-1, -1)])
        elif phase == 5:
            for index in (p2(0, 2), p2(0, 3)):
                wwait(stream, index)
            sib(stream, [(2, 0), (0, 2)])
        elif phase == 6:
            for index in (p2(2, 0), p2(2, 1)):
                wwait(stream, index)
            for index in (p2(2, 2), p2(2, 3)):
                wstart(stream, index)
        elif phase == 7:
            for index in (p2(1, 2), p2(1, 3), p2(-1, 2), p2(-1, 3)):
                wwait(stream, index)
            sib(stream, [(2, 1), (2, -1), (1, 2), (-1, 2)])
        elif phase == 8:
            for index in (p2(2, 2), p2(2, 3)):
                wwait(stream, index)
            sib(stream, [(2, 2)])
            sib_wait(stream)

    def block(source, h):
        return x_buf.at[pl.ds(POS[source] * TOK + h * SUB, SUB), :]

    ag_pending = []

    def ag_start(d, h):
        for way in (0, 1):
            if d == 7 and h != way:
                continue
            src = block((d if way == 0 else NZ - d) % NZ, h)
            dst = block(d + 1 if way == 0 else NZ - d - 1, h)
            at = (way * 8 + d) * 2 + h
            ag_pending.append(
                send(src, dst, agsend.at[at], agrecv.at[at], zr if way == 0 else zl)
            )
            pending.pop()

    def ag_wait(d, h):
        for way in (0, 1):
            if d == 7 and h != way:
                continue
            dst = block(d + 1 if way == 0 else NZ - d - 1, h)
            at = (way * 8 + d) * 2 + h
            arrived(dst, agsend.at[at], agrecv.at[at], zr if way == 0 else zl)

    def ag(i):
        d, h = i // 2, i % 2
        ag_wait(d, h)
        if d < 7:
            ag_start(d + 1, h)

    tri_r = lax.broadcasted_iota(jnp.int32, (GTOK, GTOK), 0)
    tri_c = lax.broadcasted_iota(jnp.int32, (GTOK, GTOK), 1)
    lane = lax.broadcasted_iota(jnp.int32, (8, GTOK), 1)

    def dispatch(g):
        tri = ((tri_r < tri_c) & (tri_r // TOK == tri_c // TOK)).astype(jnp.bfloat16)
        ids = ids_ref[g]
        gates = gates_ref[g]
        marks, shares = [], []
        for e in (0, 1):
            hit = ids == e * NZ + z
            marks.append(jnp.sum(hit.astype(jnp.float32), axis=0, keepdims=True))
            shares.append(jnp.sum(jnp.where(hit, gates, 0.0), axis=0, keepdims=True))
        slot_iota = lax.broadcasted_iota(jnp.int32, (GSLOT, GTOK), 0)
        picks = []
        for e in (0, 1):
            mark = jnp.broadcast_to(marks[e], (8, GTOK))
            earlier = jnp.dot(
                mark.astype(jnp.bfloat16), tri, preferred_element_type=jnp.float32
            )
            slot = jnp.where(
                mark > 0.5, earlier.astype(jnp.int32) + (lane // TOK) * CAP, -1
            )[:1]
            pick = jnp.where(slot_iota == slot, 1.0, 0.0)
            picks.append(pick)
            share = jnp.sum(pick * shares[e], axis=1, keepdims=True)
            wcol[g, pl.ds(e * GSLOT, GSLOT), :] = jnp.broadcast_to(share, (GSLOT, 128))
        pick = jnp.concatenate(picks, axis=0)
        st[g] = pick.T.astype(jnp.bfloat16)
        pick = pick.astype(jnp.bfloat16)
        b, gi = g // 2, g % 2
        for c in range(0, D, 512):
            rows = jnp.dot(
                pick,
                x_buf[pl.ds(g * GTOK, GTOK), pl.ds(c, 512)],
                preferred_element_type=jnp.float32,
            ).astype(jnp.bfloat16)
            for e in (0, 1):
                xs[b, e, pl.ds(gi * GSLOT, GSLOT), pl.ds(c, 512)] = rows[
                    e * GSLOT : (e + 1) * GSLOT
                ]

    def gate_up(b, e):
        def tile(j, carry):
            c0 = pl.multiple_of(j * 256, 256)
            c1 = pl.multiple_of(FF + j * 256, 256)
            lhs = xs[b, e]
            gate = jnp.dot(lhs, wg[e, :, pl.ds(c0, 256)], preferred_element_type=jnp.float32)
            up = jnp.dot(lhs, wg[e, :, pl.ds(c1, 256)], preferred_element_type=jnp.float32)
            hid = gate / (1.0 + jnp.exp(-gate)) * up
            act[b, e, :, pl.ds(c0, 256)] = hid.astype(jnp.bfloat16)
            return carry

        lax.fori_loop(0, FF // 256, tile, 0)

    def down(b, e):
        def tile(j, carry):
            c0 = pl.multiple_of(j * 256, 256)
            res = jnp.dot(
                act[b, e], wd[e, :, pl.ds(c0, 256)], preferred_element_type=jnp.float32
            )
            for gi in (0, 1):
                g = b * 2 + gi
                share = wcol[g, pl.ds(e * GSLOT, GSLOT), :]
                outw[g, pl.ds(e * GSLOT, GSLOT), pl.ds(c0, 256)] = (
                    res[gi * GSLOT : (gi + 1) * GSLOT]
                    * jnp.concatenate([share, share], axis=1)
                ).astype(jnp.bfloat16)
            return carry

        lax.fori_loop(0, D // 256, tile, 0)

    def spread(g):
        def tile(j, carry):
            c0 = pl.multiple_of(j * 256, 256)
            ctr[pl.ds(g * GTOK, GTOK), pl.ds(c0, 256)] = jnp.dot(
                st[g], outw[g, :, pl.ds(c0, 256)], preferred_element_type=jnp.float32
            )
            return carry

        lax.fori_loop(0, D // 256, tile, 0)

    def mine(source, h):
        return ctr[pl.ds(POS[source] * TOK + h * SUB, SUB), :]

    def rs_wait(s, way, h):
        buf = (rsr, rsl)[way].at[s - 1, pl.ds(h * SUB, SUB), :]
        at = (way * 8 + s - 1) * 2 + h
        arrived(buf, rssend.at[at], rsrecv.at[at], zr if way == 0 else zl)
        return buf

    def rs(s):
        for h in (0, 1):
            for way in (0, 1):
                if s == 0 and h != way:
                    continue
                source = 8 + s if way == 0 else 8 - s
                total = mine(source, h)
                if s > 1 or (s == 1 and h == way):
                    total = total + rs_wait(s, way, h)[...].astype(jnp.float32)
                blk = block(source, h)
                blk[...] = total.astype(jnp.bfloat16)
                at = (way * 8 + s) * 2 + h
                dst = (rsr, rsl)[way].at[s, pl.ds(h * SUB, SUB), :]
                send(blk, dst, rssend.at[at], rsrecv.at[at], zr if way == 0 else zl)

    resid = (hidden_ref[...].astype(jnp.float32) + attn_ref[...].astype(jnp.float32)).astype(
        jnp.bfloat16
    )
    resid_s[...] = resid
    resid32 = resid.astype(jnp.float32)
    mean_square = jnp.mean(resid32 * resid32, axis=-1, keepdims=True)
    x_buf[pl.ds(POS[0] * TOK, TOK), :] = (
        resid32 * lax.rsqrt(mean_square + epsilon) * gain_ref[...]
    ).astype(jnp.bfloat16)

    weights(0, 0)
    ag_start(0, 0)
    ag_start(0, 1)
    plan = [
        ("ag", 0), ("ag", 1), ("w", 0, 1), ("ag", 2), ("ag", 3), ("w", 0, 2), ("ag", 4),
        ("ag", 5), ("w", 0, 3), ("dispatch", 3), ("ag", 6), ("ag", 7), ("ag", 8), ("w", 0, 4), ("w", 1, 0),
        ("ag", 9), ("dispatch", 2), ("w", 0, 5), ("ag", 10), ("ag", 11), ("w", 0, 6), ("ag", 12), ("dispatch", 1), ("w", 0, 7),
        ("ag", 13), ("w", 1, 1), ("w", 0, 8), ("ag", 14), ("ag", 15), ("w", 1, 2), ("gate_up", 1, 0),
        ("w", 1, 3), ("dispatch", 0), ("w", 1, 4), ("gate_up", 1, 1), ("w", 1, 5), ("w", 1, 6),
        ("gate_up", 0, 0), ("w", 1, 7), ("gate_up", 0, 1), ("w", 1, 8), ("agdone",),
        ("down", 0, 0), ("down", 0, 1), ("spread", 0), ("rs", 0), ("rs", 1), ("spread", 1), ("rs", 2),
        ("down", 1, 0), ("rs", 3), ("down", 1, 1), ("spread", 2), ("rs", 4), ("spread", 3),
        ("rs", 5), ("rs", 6), ("rs", 7),
    ]

    def ag_done():
        for copy in ag_pending:
            copy.wait_send()

    run = {
        "ag": ag, "w": weights, "dispatch": dispatch, "gate_up": gate_up, "down": down,
        "spread": spread, "rs": rs, "agdone": ag_done,
    }
    for name, *args in plan:
        run[name](*args)

    for h in (0, 1):
        total = resid_s[pl.ds(h * SUB, SUB), :].astype(jnp.float32) + mine(0, h)
        for way in (0, 1):
            total = total + rs_wait(8, way, h)[...].astype(jnp.float32)
        out_ref[pl.ds(h * SUB, SUB), :] = total.astype(jnp.bfloat16)
    for copy in pending:
        copy.wait_send()


def moe(hidden, attn, gain, ids, gates, gate_up, down):
    vmem = pl.BlockSpec(memory_space=pltpu.VMEM)
    hbm = pl.BlockSpec(memory_space=pl.ANY)
    bf, f32 = jnp.bfloat16, jnp.float32
    dma = pltpu.SemaphoreType.DMA
    return pl.pallas_call(
        moe_kernel,
        out_shape=jax.ShapeDtypeStruct((TOK, D), bf),
        in_specs=[vmem] * 5 + [hbm] * 2,
        out_specs=vmem,
        scratch_shapes=[
            pltpu.VMEM((NZ * TOK, D), bf),
            pltpu.VMEM((2, D, 2 * FF), bf),
            pltpu.VMEM((2, FF, D), bf),
            pltpu.VMEM((ROWS[0], D), f32),
            pltpu.VMEM((ROWS[1], D), f32),
            pltpu.VMEM((2, 2, 2 * GSLOT, D), bf),
            pltpu.VMEM((2, 2, 2 * GSLOT, FF), bf),
            pltpu.VMEM((NGRP, 2 * GSLOT, D), bf),
            pltpu.VMEM((NGRP, 2 * GSLOT, 128), f32),
            pltpu.VMEM((NGRP, GTOK, 2 * GSLOT), bf),
            pltpu.VMEM((NZ * TOK, D), f32),
            pltpu.VMEM((8, TOK, D), bf),
            pltpu.VMEM((8, TOK, D), bf),
            pltpu.VMEM((TOK, D), bf),
            dma((2,)),
            dma((4 * NMSG,)),
            dma((4 * NMSG,)),
            dma((32,)),
            dma((32,)),
            dma((32,)),
            dma((32,)),
            dma((32,)),
            dma((32,)),
        ],
        compiler_params=pltpu.CompilerParams(
            collective_id=0, has_side_effects=True, vmem_limit_bytes=56 * 1024 * 1024
        ),
    )(hidden, attn, gain, ids, gates, gate_up, down)


def attention_kernel(table_ref, length_ref, q_ref, k_ref, v_ref, out_ref, keys, values):
    for p in range(PAGES):
        at = table_ref[0, p]
        keys[pl.ds(p * PAGE, PAGE), :] = k_ref[at]
        values[pl.ds(p * PAGE, PAGE), :] = v_ref[at]
    scale = 1.0 / math.sqrt(HDIM)
    key_at = lax.broadcasted_iota(jnp.int32, (1, COL), 1)
    end = jnp.int32(0)
    ends = []
    for r in range(REQS):
        end = end + length_ref[0, r]
        ends.append(end)
    key_request = sum((key_at >= e).astype(jnp.int32) for e in ends)

    def block(i, carry):
        first = pl.multiple_of(i * QROWS, QROWS)
        row_at = first + lax.broadcasted_iota(jnp.int32, (QROWS, 1), 0)
        row_request = sum((row_at >= e).astype(jnp.int32) for e in ends)
        scores = (
            lax.dot_general(
                q_ref[pl.ds(first, QROWS), :],
                keys[...],
                (((1,), (1,)), ((), ())),
                preferred_element_type=jnp.float32,
            )
            * scale
        )
        scores = jnp.where(row_request == key_request, scores, -1e30)
        highest = jnp.max(scores, axis=-1, keepdims=True)
        weights = jnp.exp(scores - highest)
        totals = jnp.sum(weights, axis=-1, keepdims=True)
        probs = (weights * (1.0 / totals)).astype(jnp.bfloat16)
        out_ref[pl.ds(first, QROWS), :] = jnp.dot(
            probs, values[...], preferred_element_type=jnp.float32
        ).astype(jnp.bfloat16)
        return carry

    lax.fori_loop(0, COL // QROWS, block, 0)


def attention(queries, key_pool, value_pool, page_table, prompt_lengths):
    vmem = pl.BlockSpec(memory_space=pltpu.VMEM)
    smem = pl.BlockSpec(memory_space=pltpu.SMEM)
    return pl.pallas_call(
        attention_kernel,
        out_shape=jax.ShapeDtypeStruct((COL, HDIM), jnp.bfloat16),
        in_specs=[smem, smem, vmem, vmem, vmem],
        out_specs=vmem,
        scratch_shapes=[
            pltpu.VMEM((COL, HDIM), jnp.bfloat16),
            pltpu.VMEM((COL, HDIM), jnp.bfloat16),
        ],
        compiler_params=pltpu.CompilerParams(vmem_limit_bytes=16 * 1024 * 1024),
    )(page_table, prompt_lengths, queries, key_pool, value_pool)


def local(
    hidden_in,
    queries,
    key_pool,
    value_pool,
    page_table,
    prompt_lengths,
    expert_ids,
    gate_weights,
    norm_gain,
    trainer_gate_up,
    trainer_down,
):
    routing = jnp.concatenate([expert_ids[0].astype(jnp.float32), gate_weights[0]], axis=1)
    rings = [[half * NZ + k for k in range(NZ)] for half in range(2)]
    routing = lax.all_gather(routing.T, "expert", axis_index_groups=rings)
    z = lax.axis_index("expert") % NZ
    behind = lax.rev(routing, (0,))
    behind = jnp.concatenate([behind, behind], axis=0)
    behind = lax.dynamic_slice_in_dim(behind, NZ - 1 - z, NZ, axis=0)
    routing = jnp.stack(
        [
            jnp.concatenate([behind[s] for s in ORDER[g * GRP : (g + 1) * GRP]], axis=1)
            for g in range(NGRP)
        ]
    )
    ids, gates = routing[:, :TOPK].astype(jnp.int32), routing[:, TOPK:]

    attn_heads = attention(queries[0], key_pool, value_pool, page_table, prompt_lengths)
    attn_tokens = lax.all_to_all(attn_heads[None], "dp", split_axis=1, concat_axis=2, tiled=True)
    mixed = moe(
        hidden_in[0],
        attn_tokens[0],
        norm_gain[None],
        ids,
        gates,
        trainer_gate_up[0],
        trainer_down[0],
    )
    return mixed[None]


def solution(mesh):
    placed = (
        P("expert", "dp", None),
        P("expert", None, "dp"),
        P("expert", None, "dp"),
        P("expert", None, "dp"),
        P("expert", None),
        P("expert", None),
        P("expert", "dp", None),
        P("expert", "dp", None),
        P(),
        P("expert", "dp", None),
        P("expert", "dp", None),
    )
    return jax.shard_map(
        local, mesh=mesh, in_specs=placed, out_specs=P("expert", "dp", None), check_vma=False
    )
```

```python
import math

import jax
import jax.numpy as jnp
from jax import lax
from jax.experimental import pallas as pl
from jax.experimental.pallas import tpu as pltpu
from jax.sharding import PartitionSpec as P

MESH = pl.DeviceIdType.MESH
HDIM = 128
TOPK = 8
D = 2048
FF = 1024
NZ = 16
NDP = 16
TOK = 64
SUB = TOK // 2
CAP = 20
GRP = 4
GSLOT = GRP * CAP
GTOK = GRP * TOK
NGRP = NZ // GRP
COL = 1024
PAGE = 128
PAGES = COL // PAGE
REQS = 4
QROWS = 256
epsilon = 1e-05

ORDER = (8, 7, 9, 6, 10, 5, 11, 4, 12, 3, 13, 2, 14, 1, 15, 0)
POS = {s: i for i, s in enumerate(ORDER)}

ROWS = (128, 64)
KS = (0, 1, -1, 2)
NMSG = 4 + 4 * len(KS)


def moe_kernel(
    table_ref,
    length_ref,
    q_ref,
    k_ref,
    v_ref,
    hidden_ref,
    gain_ref,
    routing_ref,
    gu_hbm,
    dn_hbm,
    out_ref,
    keys,
    values,
    heads_out,
    heads_in,
    route,
    x_buf,
    wg,
    wd,
    gu32,
    dn32,
    xs,
    act,
    outw,
    wcol,
    st,
    ctr,
    rsr,
    rsl,
    resid_s,
    load_sem,
    wsend,
    wrecv,
    sibsend,
    sibrecv,
    agsend,
    agrecv,
    rssend,
    rsrecv,
    hsend,
    hrecv,
    rtsend,
    rtrecv,
):
    dp = lax.axis_index("dp")
    ex = lax.axis_index("expert")
    x = dp // 4
    y = ((dp // 2) % 2) * 2 + ex // NZ
    core = dp % 2
    z = ex % NZ

    def dev(xx, yy, zz, cc):
        return ((xx * 2 + yy // 2) * 2 + cc, (yy % 2) * NZ + zz)

    def ring4(v, k):
        return (v + 4 + k) % 4

    sibling = dev(x, y, z, 1 - core)
    zr = dev(x, y, (z + 1) % NZ, core)
    zl = dev(x, y, (z + NZ - 1) % NZ, core)
    xy = {
        (0, 1): dev(ring4(x, 1), y, z, core),
        (0, -1): dev(ring4(x, -1), y, z, core),
        (1, 1): dev(x, ring4(y, 1), z, core),
        (1, -1): dev(x, ring4(y, -1), z, core),
    }

    load_gu = pltpu.make_async_copy(gu_hbm, gu32, load_sem.at[0])
    load_dn = pltpu.make_async_copy(dn_hbm, dn32, load_sem.at[1])
    load_gu.start()
    load_dn.start()

    barrier = pltpu.get_barrier_semaphore()
    peers = [((dp + k) % NDP, ex) for k in range(1, NDP)]
    partners = peers + [zr, zl, xy[1, 1], xy[1, -1]]
    for partner in partners:
        pl.semaphore_signal(barrier, inc=1, device_id=partner, device_id_type=MESH)

    pending = []

    def send(src, dst, ssem, rsem, to):
        copy = pltpu.make_async_remote_copy(
            src_ref=src,
            dst_ref=dst,
            send_sem=ssem,
            recv_sem=rsem,
            device_id=to,
            device_id_type=MESH,
        )
        copy.start()
        pending.append(copy)
        return copy

    def arrived(ref, ssem, rsem, to):
        pltpu.make_async_remote_copy(
            src_ref=ref,
            dst_ref=ref,
            send_sem=ssem,
            recv_sem=rsem,
            device_id=to,
            device_id_type=MESH,
        ).wait_recv()

    def shard(stream, dx, dy, off, n):
        sx, sy = ring4(x, -dx), ring4(y, -dy)
        rows = ROWS[stream]
        first = pl.multiple_of(((sx * 2 + sy // 2) * 2 + core) * rows + off, 16)
        buf = wd if stream else wg
        return buf.at[sy % 2, pl.ds(first, n), :]

    def piece(stream, half, k1, k2, part):
        h = ROWS[stream] // 2
        q = h // 2
        off, n = (half * h, h) if part is None else (half * h + part * q, q)
        dx, dy = (k1, k2) if half == 0 else (k2, k1)
        return shard(stream, dx, dy, off, n)

    def wmsg(stream, half, index):
        at = (stream * 2 + half) * NMSG + index
        return wsend.at[at], wrecv.at[at]

    def decode(index):
        if index < 4:
            return 0, (1, -1)[index % 2], index >= 2, 0
        return 1, (1, -1)[index % 2], (index - 4) % 4 >= 2, KS[(index - 4) // 4]

    def wstart(stream, index):
        ring, sign, forward, k = decode(index)
        for half in (0, 1):
            axis = ring if half == 0 else 1 - ring
            part = (0 if sign == 1 else 1) if forward else None
            step = sign if forward else 0
            k1, k2 = (step, 0) if ring == 0 else (k, step)
            ref = piece(stream, half, k1, k2, part)
            ssem, rsem = wmsg(stream, half, index)
            send(ref, ref, ssem, rsem, xy[axis, sign])

    def wwait(stream, index):
        ring, sign, forward, k = decode(index)
        for half in (0, 1):
            axis = ring if half == 0 else 1 - ring
            part = (0 if sign == 1 else 1) if forward else None
            step = 2 if forward else sign
            k1, k2 = (step, 0) if ring == 0 else (k, step)
            ref = piece(stream, half, k1, k2, part)
            ssem, rsem = wmsg(stream, half, index)
            arrived(ref, ssem, rsem, xy[axis, sign])

    def p2(k, j):
        return 4 + 4 * KS.index(k) + j

    sib_index = {}

    def sib(stream, places):
        for dx, dy in places:
            at = stream * 16 + (dx % 4) * 4 + (dy % 4)
            ref = shard(stream, dx, dy, 0, ROWS[stream])
            send(ref, ref, sibsend.at[at], sibrecv.at[at], sibling)
            sib_index[at] = (stream, dx, dy)

    def sib_wait(stream):
        for at, (s, dx, dy) in sib_index.items():
            if s == stream:
                sx, sy = ring4(x, -dx), ring4(y, -dy)
                rows = ROWS[stream]
                first = pl.multiple_of(((sx * 2 + sy // 2) * 2 + 1 - core) * rows, 16)
                buf = wd if stream else wg
                ref = buf.at[sy % 2, pl.ds(first, rows), :]
                arrived(ref, sibsend.at[at], sibrecv.at[at], sibling)

    def weights(stream, phase):
        if phase == 0:
            (load_gu, load_dn)[stream].wait()
            src = (gu32, dn32)[stream]
            rows = ROWS[stream]
            first = pl.multiple_of(dp * rows, 16)
            (wg, wd)[stream][y % 2, pl.ds(first, rows), :] = src[...].astype(jnp.bfloat16)
            if stream == 0:
                pl.semaphore_wait(barrier, len(partners))
            for index in (0, 1, p2(0, 0), p2(0, 1)):
                wstart(stream, index)
            sib(stream, [(0, 0)])
        elif phase == 1:
            for index in (0, 1):
                wwait(stream, index)
            for index in (2, 3, p2(1, 0), p2(1, 1), p2(-1, 0), p2(-1, 1)):
                wstart(stream, index)
        elif phase == 2:
            for index in (p2(0, 0), p2(0, 1)):
                wwait(stream, index)
            for index in (p2(0, 2), p2(0, 3)):
                wstart(stream, index)
            sib(stream, [(1, 0), (-1, 0), (0, 1), (0, -1)])
        elif phase == 3:
            for index in (2, 3):
                wwait(stream, index)
            for index in (p2(2, 0), p2(2, 1)):
                wstart(stream, index)
        elif phase == 4:
            for index in (p2(1, 0), p2(1, 1), p2(-1, 0), p2(-1, 1)):
                wwait(stream, index)
            for index in (p2(1, 2), p2(1, 3), p2(-1, 2), p2(-1, 3)):
                wstart(stream, index)
            sib(stream, [(1, 1), (-1, 1), (1, -1), (-1, -1)])
        elif phase == 5:
            for index in (p2(0, 2), p2(0, 3)):
                wwait(stream, index)
            sib(stream, [(2, 0), (0, 2)])
        elif phase == 6:
            for index in (p2(2, 0), p2(2, 1)):
                wwait(stream, index)
            for index in (p2(2, 2), p2(2, 3)):
                wstart(stream, index)
        elif phase == 7:
            for index in (p2(1, 2), p2(1, 3), p2(-1, 2), p2(-1, 3)):
                wwait(stream, index)
            sib(stream, [(2, 1), (2, -1), (1, 2), (-1, 2)])
        elif phase == 8:
            for index in (p2(2, 2), p2(2, 3)):
                wwait(stream, index)
            sib(stream, [(2, 2)])
            sib_wait(stream)

    def block(source, h):
        return x_buf.at[pl.ds(POS[source] * TOK + h * SUB, SUB), :]

    ag_pending = []

    def ag_start(d, h):
        for way in (0, 1):
            if d == 7 and h != way:
                continue
            src = block((d if way == 0 else NZ - d) % NZ, h)
            dst = block(d + 1 if way == 0 else NZ - d - 1, h)
            at = (way * 8 + d) * 2 + h
            ag_pending.append(
                send(src, dst, agsend.at[at], agrecv.at[at], zr if way == 0 else zl)
            )
            pending.pop()
            if h == 0 and not (d == 7 and way == 1):
                at = way * 8 + d
                send(
                    route.at[(d if way == 0 else NZ - d) % NZ],
                    route.at[d + 1 if way == 0 else NZ - d - 1],
                    rtsend.at[at],
                    rtrecv.at[at],
                    zr if way == 0 else zl,
                )

    def ag_wait(d, h):
        for way in (0, 1):
            if d == 7 and h != way:
                continue
            dst = block(d + 1 if way == 0 else NZ - d - 1, h)
            at = (way * 8 + d) * 2 + h
            arrived(dst, agsend.at[at], agrecv.at[at], zr if way == 0 else zl)
            if h == 0 and not (d == 7 and way == 1):
                at = way * 8 + d
                arrived(
                    route.at[d + 1 if way == 0 else NZ - d - 1],
                    rtsend.at[at],
                    rtrecv.at[at],
                    zr if way == 0 else zl,
                )

    def ag(i):
        d, h = i // 2, i % 2
        ag_wait(d, h)
        if d < 7:
            ag_start(d + 1, h)

    tri_r = lax.broadcasted_iota(jnp.int32, (GTOK, GTOK), 0)
    tri_c = lax.broadcasted_iota(jnp.int32, (GTOK, GTOK), 1)
    lane = lax.broadcasted_iota(jnp.int32, (8, GTOK), 1)

    def dispatch(g):
        tri = ((tri_r < tri_c) & (tri_r // TOK == tri_c // TOK)).astype(jnp.bfloat16)
        parts = [route[s] for s in ORDER[g * GRP : (g + 1) * GRP]]
        parts = jnp.concatenate([part[:, :TOK] for part in parts], axis=1)
        ids, gates = parts[:TOPK], parts[TOPK:]
        marks, shares = [], []
        for e in (0, 1):
            hit = ids == (e * NZ + z).astype(jnp.float32)
            marks.append(jnp.sum(hit.astype(jnp.float32), axis=0, keepdims=True))
            shares.append(jnp.sum(jnp.where(hit, gates, 0.0), axis=0, keepdims=True))
        slot_iota = lax.broadcasted_iota(jnp.int32, (GSLOT, GTOK), 0)
        picks = []
        for e in (0, 1):
            mark = jnp.broadcast_to(marks[e], (8, GTOK))
            earlier = jnp.dot(
                mark.astype(jnp.bfloat16), tri, preferred_element_type=jnp.float32
            )
            slot = jnp.where(
                mark > 0.5, earlier.astype(jnp.int32) + (lane // TOK) * CAP, -1
            )[:1]
            pick = jnp.where(slot_iota == slot, 1.0, 0.0)
            picks.append(pick)
            share = jnp.sum(pick * shares[e], axis=1, keepdims=True)
            wcol[g, pl.ds(e * GSLOT, GSLOT), :] = jnp.broadcast_to(share, (GSLOT, 128))
        pick = jnp.concatenate(picks, axis=0)
        st[g] = pick.T.astype(jnp.bfloat16)
        pick = pick.astype(jnp.bfloat16)
        b, gi = g // 2, g % 2
        for c in range(0, D, 512):
            rows = jnp.dot(
                pick,
                x_buf[pl.ds(g * GTOK, GTOK), pl.ds(c, 512)],
                preferred_element_type=jnp.float32,
            ).astype(jnp.bfloat16)
            for e in (0, 1):
                xs[b, e, pl.ds(gi * GSLOT, GSLOT), pl.ds(c, 512)] = rows[
                    e * GSLOT : (e + 1) * GSLOT
                ]

    def gate_up(b, e):
        def tile(j, carry):
            c0 = pl.multiple_of(j * 256, 256)
            c1 = pl.multiple_of(FF + j * 256, 256)
            lhs = xs[b, e]
            gate = jnp.dot(lhs, wg[e, :, pl.ds(c0, 256)], preferred_element_type=jnp.float32)
            up = jnp.dot(lhs, wg[e, :, pl.ds(c1, 256)], preferred_element_type=jnp.float32)
            hid = gate / (1.0 + jnp.exp(-gate)) * up
            act[b, e, :, pl.ds(c0, 256)] = hid.astype(jnp.bfloat16)
            return carry

        lax.fori_loop(0, FF // 256, tile, 0)

    def down(b, e):
        def tile(j, carry):
            c0 = pl.multiple_of(j * 256, 256)
            res = jnp.dot(
                act[b, e], wd[e, :, pl.ds(c0, 256)], preferred_element_type=jnp.float32
            )
            for gi in (0, 1):
                g = b * 2 + gi
                share = wcol[g, pl.ds(e * GSLOT, GSLOT), :]
                outw[g, pl.ds(e * GSLOT, GSLOT), pl.ds(c0, 256)] = (
                    res[gi * GSLOT : (gi + 1) * GSLOT]
                    * jnp.concatenate([share, share], axis=1)
                ).astype(jnp.bfloat16)
            return carry

        lax.fori_loop(0, D // 256, tile, 0)

    def spread(g):
        def tile(j, carry):
            c0 = pl.multiple_of(j * 256, 256)
            ctr[pl.ds(g * GTOK, GTOK), pl.ds(c0, 256)] = jnp.dot(
                st[g], outw[g, :, pl.ds(c0, 256)], preferred_element_type=jnp.float32
            )
            return carry

        lax.fori_loop(0, D // 256, tile, 0)

    def mine(source, h):
        return ctr[pl.ds(POS[source] * TOK + h * SUB, SUB), :]

    def rs_wait(s, way, h):
        buf = (rsr, rsl)[way].at[s - 1, pl.ds(h * SUB, SUB), :]
        at = (way * 8 + s - 1) * 2 + h
        arrived(buf, rssend.at[at], rsrecv.at[at], zr if way == 0 else zl)
        return buf

    def rs(s):
        for h in (0, 1):
            for way in (0, 1):
                if s == 0 and h != way:
                    continue
                source = 8 + s if way == 0 else 8 - s
                total = mine(source, h)
                if s > 1 or (s == 1 and h == way):
                    total = total + rs_wait(s, way, h)[...].astype(jnp.float32)
                blk = block(source, h)
                blk[...] = total.astype(jnp.bfloat16)
                at = (way * 8 + s) * 2 + h
                dst = (rsr, rsl)[way].at[s, pl.ds(h * SUB, SUB), :]
                send(blk, dst, rssend.at[at], rsrecv.at[at], zr if way == 0 else zl)

    route[0] = routing_ref[...]
    weights(0, 0)

    for p in range(PAGES):
        at = table_ref[0, p]
        keys[pl.ds(p * PAGE, PAGE), :] = k_ref[at]
        values[pl.ds(p * PAGE, PAGE), :] = v_ref[at]
    scale = 1.0 / math.sqrt(HDIM)
    key_at = lax.broadcasted_iota(jnp.int32, (1, COL), 1)
    end = jnp.int32(0)
    ends = []
    for r in range(REQS):
        end = end + length_ref[0, r]
        ends.append(end)
    key_request = sum((key_at >= e).astype(jnp.int32) for e in ends)

    def attend(i, carry):
        first = pl.multiple_of(i * QROWS, QROWS)
        row_at = first + lax.broadcasted_iota(jnp.int32, (QROWS, 1), 0)
        row_request = sum((row_at >= e).astype(jnp.int32) for e in ends)
        scores = (
            lax.dot_general(
                q_ref[pl.ds(first, QROWS), :],
                keys[...],
                (((1,), (1,)), ((), ())),
                preferred_element_type=jnp.float32,
            )
            * scale
        )
        scores = jnp.where(row_request == key_request, scores, -1e30)
        highest = jnp.max(scores, axis=-1, keepdims=True)
        share = jnp.exp(scores - highest)
        totals = jnp.sum(share, axis=-1, keepdims=True)
        probs = (share * (1.0 / totals)).astype(jnp.bfloat16)
        heads_out[pl.ds(first, QROWS), :] = jnp.dot(
            probs, values[...], preferred_element_type=jnp.float32
        ).astype(jnp.bfloat16)
        return carry

    lax.fori_loop(0, COL // QROWS, attend, 0)
    for k in range(1, NDP):
        to = (dp + k) % NDP
        send(
            heads_out.at[pl.ds(pl.multiple_of(to * TOK, TOK), TOK), :],
            heads_in.at[k],
            hsend.at[k],
            hrecv.at[k],
            peers[k - 1],
        )
    heads_in[0] = heads_out[pl.ds(pl.multiple_of(dp * TOK, TOK), TOK), :]
    weights(0, 1)
    for k in range(1, NDP):
        arrived(heads_in.at[k], hsend.at[k], hrecv.at[k], peers[k - 1])
    squares = jnp.zeros((TOK, HDIM), jnp.float32)
    for h in range(NDP):
        cols = pl.ds(h * HDIM, HDIM)
        attn = heads_in[(dp + NDP - h) % NDP].astype(jnp.float32)
        resid = (hidden_ref[:, cols].astype(jnp.float32) + attn).astype(jnp.bfloat16)
        resid_s[:, cols] = resid
        squares = squares + resid.astype(jnp.float32) * resid.astype(jnp.float32)
    factor = lax.rsqrt(jnp.sum(squares, axis=-1, keepdims=True) * (1.0 / D) + epsilon)
    x_buf[pl.ds(POS[0] * TOK, TOK), :] = (
        resid_s[...].astype(jnp.float32) * factor * gain_ref[...]
    ).astype(jnp.bfloat16)

    ag_start(0, 0)
    ag_start(0, 1)
    plan = [
        ("ag", 0), ("ag", 1), ("ag", 2), ("ag", 3), ("w", 0, 2), ("ag", 4),
        ("ag", 5), ("w", 0, 3), ("dispatch", 3), ("ag", 6), ("ag", 7), ("ag", 8), ("w", 0, 4), ("w", 1, 0),
        ("ag", 9), ("dispatch", 2), ("w", 0, 5), ("ag", 10), ("ag", 11), ("w", 0, 6), ("ag", 12), ("dispatch", 1), ("w", 0, 7),
        ("ag", 13), ("w", 1, 1), ("w", 0, 8), ("ag", 14), ("ag", 15), ("w", 1, 2), ("gate_up", 1, 0),
        ("w", 1, 3), ("dispatch", 0), ("w", 1, 4), ("gate_up", 1, 1), ("w", 1, 5), ("w", 1, 6),
        ("gate_up", 0, 0), ("w", 1, 7), ("gate_up", 0, 1), ("w", 1, 8), ("agdone",),
        ("down", 0, 0), ("down", 0, 1), ("spread", 0), ("rs", 0), ("rs", 1), ("spread", 1), ("rs", 2),
        ("down", 1, 0), ("rs", 3), ("down", 1, 1), ("spread", 2), ("rs", 4), ("spread", 3),
        ("rs", 5), ("rs", 6), ("rs", 7),
    ]

    def ag_done():
        for copy in ag_pending:
            copy.wait_send()

    run = {
        "ag": ag, "w": weights, "dispatch": dispatch, "gate_up": gate_up, "down": down,
        "spread": spread, "rs": rs, "agdone": ag_done,
    }
    for name, *args in plan:
        run[name](*args)

    for h in (0, 1):
        total = resid_s[pl.ds(h * SUB, SUB), :].astype(jnp.float32) + mine(0, h)
        for way in (0, 1):
            total = total + rs_wait(8, way, h)[...].astype(jnp.float32)
        out_ref[pl.ds(h * SUB, SUB), :] = total.astype(jnp.bfloat16)
    for copy in pending:
        copy.wait_send()


def moe(table, lengths, queries, keys, values, hidden, gain, routing, gate_up, down):
    vmem = pl.BlockSpec(memory_space=pltpu.VMEM)
    smem = pl.BlockSpec(memory_space=pltpu.SMEM)
    hbm = pl.BlockSpec(memory_space=pl.ANY)
    bf, f32 = jnp.bfloat16, jnp.float32
    dma = pltpu.SemaphoreType.DMA
    return pl.pallas_call(
        moe_kernel,
        out_shape=jax.ShapeDtypeStruct((TOK, D), bf),
        in_specs=[smem] * 2 + [vmem] * 6 + [hbm] * 2,
        out_specs=vmem,
        scratch_shapes=[
            pltpu.VMEM((COL, HDIM), bf),
            pltpu.VMEM((COL, HDIM), bf),
            pltpu.VMEM((COL, HDIM), bf),
            pltpu.VMEM((NDP, TOK, HDIM), bf),
            pltpu.VMEM((NZ, 2 * TOPK, 2 * TOK), f32),
            pltpu.VMEM((NZ * TOK, D), bf),
            pltpu.VMEM((2, D, 2 * FF), bf),
            pltpu.VMEM((2, FF, D), bf),
            pltpu.VMEM((ROWS[0], D), f32),
            pltpu.VMEM((ROWS[1], D), f32),
            pltpu.VMEM((2, 2, 2 * GSLOT, D), bf),
            pltpu.VMEM((2, 2, 2 * GSLOT, FF), bf),
            pltpu.VMEM((NGRP, 2 * GSLOT, D), bf),
            pltpu.VMEM((NGRP, 2 * GSLOT, 128), f32),
            pltpu.VMEM((NGRP, GTOK, 2 * GSLOT), bf),
            pltpu.VMEM((NZ * TOK, D), f32),
            pltpu.VMEM((8, TOK, D), bf),
            pltpu.VMEM((8, TOK, D), bf),
            pltpu.VMEM((TOK, D), bf),
            dma((2,)),
            dma((4 * NMSG,)),
            dma((4 * NMSG,)),
            dma((32,)),
            dma((32,)),
            dma((32,)),
            dma((32,)),
            dma((32,)),
            dma((32,)),
            dma((NDP,)),
            dma((NDP,)),
            dma((16,)),
            dma((16,)),
        ],
        compiler_params=pltpu.CompilerParams(
            collective_id=0, has_side_effects=True, vmem_limit_bytes=56 * 1024 * 1024
        ),
    )(table, lengths, queries, keys, values, hidden, gain, routing, gate_up, down)


def local(
    hidden_in,
    queries,
    key_pool,
    value_pool,
    page_table,
    prompt_lengths,
    expert_ids,
    gate_weights,
    norm_gain,
    trainer_gate_up,
    trainer_down,
):
    routing = jnp.concatenate([expert_ids[0].astype(jnp.float32), gate_weights[0]], axis=1)
    routing = jnp.pad(routing.T, ((0, 0), (0, TOK)))
    mixed = moe(
        page_table,
        prompt_lengths,
        queries[0],
        key_pool,
        value_pool,
        hidden_in[0],
        norm_gain[None],
        routing,
        trainer_gate_up[0],
        trainer_down[0],
    )
    return mixed[None]


def solution(mesh):
    placed = (
        P("expert", "dp", None),
        P("expert", None, "dp"),
        P("expert", None, "dp"),
        P("expert", None, "dp"),
        P("expert", None),
        P("expert", None),
        P("expert", "dp", None),
        P("expert", "dp", None),
        P(),
        P("expert", "dp", None),
        P("expert", "dp", None),
    )
    return jax.shard_map(
        local, mesh=mesh, in_specs=placed, out_specs=P("expert", "dp", None), check_vma=False
    )
```

```python
import math

import jax
import jax.numpy as jnp
from jax import lax
from jax.experimental import pallas as pl
from jax.experimental.pallas import tpu as pltpu
from jax.sharding import PartitionSpec as P

MESH = pl.DeviceIdType.MESH
HDIM = 128
TOPK = 8
D = 2048
FF = 1024
NZ = 16
NDP = 16
TOK = 64
SUB = TOK // 2
CAP = 20
GRP = 4
GSLOT = GRP * CAP
GTOK = GRP * TOK
NGRP = NZ // GRP
WIDE = 512
HALF = D // 2
COL = 1024
PAGE = 128
PAGES = COL // PAGE
REQS = 4
QROWS = 256
epsilon = 1e-05

ORDER = (8, 7, 9, 6, 10, 5, 11, 4, 12, 3, 13, 2, 14, 1, 15, 0)
POS = {s: i for i, s in enumerate(ORDER)}

ROWS = (128, 64)
KS = (0, 1, -1, 2)
NMSG = 4 + 4 * len(KS)


def moe_kernel(
    table_ref,
    length_ref,
    q_ref,
    k_ref,
    v_ref,
    hidden_ref,
    gain_ref,
    routing_ref,
    gu_hbm,
    dn_hbm,
    out_ref,
    keys,
    values,
    heads_out,
    heads_in,
    route,
    x_buf,
    wg,
    wd,
    gu32,
    dn32,
    xs,
    act,
    outw,
    wcol,
    st,
    ctr,
    rsr,
    rsl,
    resid_s,
    load_sem,
    wsend,
    wrecv,
    sibsend,
    sibrecv,
    agsend,
    agrecv,
    rssend,
    rsrecv,
    hsend,
    hrecv,
    rtsend,
    rtrecv,
):
    dp = lax.axis_index("dp")
    ex = lax.axis_index("expert")
    x = dp // 4
    y = ((dp // 2) % 2) * 2 + ex // NZ
    core = dp % 2
    z = ex % NZ

    def dev(xx, yy, zz, cc):
        return ((xx * 2 + yy // 2) * 2 + cc, (yy % 2) * NZ + zz)

    def ring4(v, k):
        return (v + 4 + k) % 4

    sibling = dev(x, y, z, 1 - core)
    zr = dev(x, y, (z + 1) % NZ, core)
    zl = dev(x, y, (z + NZ - 1) % NZ, core)
    xy = {
        (0, 1): dev(ring4(x, 1), y, z, core),
        (0, -1): dev(ring4(x, -1), y, z, core),
        (1, 1): dev(x, ring4(y, 1), z, core),
        (1, -1): dev(x, ring4(y, -1), z, core),
    }

    load_gu = pltpu.make_async_copy(gu_hbm, gu32, load_sem.at[0])
    load_dn = pltpu.make_async_copy(dn_hbm, dn32, load_sem.at[1])
    load_gu.start()
    load_dn.start()

    barrier = pltpu.get_barrier_semaphore()
    peers = [((dp + k) % NDP, ex) for k in range(1, NDP)]
    partners = peers + [zr, zl, xy[1, 1], xy[1, -1]]
    for partner in partners:
        pl.semaphore_signal(barrier, inc=1, device_id=partner, device_id_type=MESH)

    pending = []

    def send(src, dst, ssem, rsem, to):
        copy = pltpu.make_async_remote_copy(
            src_ref=src,
            dst_ref=dst,
            send_sem=ssem,
            recv_sem=rsem,
            device_id=to,
            device_id_type=MESH,
        )
        copy.start()
        pending.append(copy)
        return copy

    def arrived(ref, ssem, rsem, to):
        pltpu.make_async_remote_copy(
            src_ref=ref,
            dst_ref=ref,
            send_sem=ssem,
            recv_sem=rsem,
            device_id=to,
            device_id_type=MESH,
        ).wait_recv()

    def shard(stream, dx, dy, off, n):
        sx, sy = ring4(x, -dx), ring4(y, -dy)
        rows = ROWS[stream]
        first = pl.multiple_of(((sx * 2 + sy // 2) * 2 + core) * rows + off, 16)
        buf = wd if stream else wg
        return buf.at[sy % 2, pl.ds(first, n), :]

    def piece(stream, half, k1, k2, part):
        h = ROWS[stream] // 2
        q = h // 2
        off, n = (half * h, h) if part is None else (half * h + part * q, q)
        dx, dy = (k1, k2) if half == 0 else (k2, k1)
        return shard(stream, dx, dy, off, n)

    def wmsg(stream, half, index):
        at = (stream * 2 + half) * NMSG + index
        return wsend.at[at], wrecv.at[at]

    def decode(index):
        if index < 4:
            return 0, (1, -1)[index % 2], index >= 2, 0
        return 1, (1, -1)[index % 2], (index - 4) % 4 >= 2, KS[(index - 4) // 4]

    def wstart(stream, index):
        ring, sign, forward, k = decode(index)
        for half in (0, 1):
            axis = ring if half == 0 else 1 - ring
            part = (0 if sign == 1 else 1) if forward else None
            step = sign if forward else 0
            k1, k2 = (step, 0) if ring == 0 else (k, step)
            ref = piece(stream, half, k1, k2, part)
            ssem, rsem = wmsg(stream, half, index)
            send(ref, ref, ssem, rsem, xy[axis, sign])

    def wwait(stream, index):
        ring, sign, forward, k = decode(index)
        for half in (0, 1):
            axis = ring if half == 0 else 1 - ring
            part = (0 if sign == 1 else 1) if forward else None
            step = 2 if forward else sign
            k1, k2 = (step, 0) if ring == 0 else (k, step)
            ref = piece(stream, half, k1, k2, part)
            ssem, rsem = wmsg(stream, half, index)
            arrived(ref, ssem, rsem, xy[axis, sign])

    def p2(k, j):
        return 4 + 4 * KS.index(k) + j

    sib_index = {}

    def sib(stream, places):
        for dx, dy in places:
            at = stream * 16 + (dx % 4) * 4 + (dy % 4)
            ref = shard(stream, dx, dy, 0, ROWS[stream])
            send(ref, ref, sibsend.at[at], sibrecv.at[at], sibling)
            sib_index[at] = (stream, dx, dy)

    def sib_wait(stream):
        for at, (s, dx, dy) in sib_index.items():
            if s == stream:
                sx, sy = ring4(x, -dx), ring4(y, -dy)
                rows = ROWS[stream]
                first = pl.multiple_of(((sx * 2 + sy // 2) * 2 + 1 - core) * rows, 16)
                buf = wd if stream else wg
                ref = buf.at[sy % 2, pl.ds(first, rows), :]
                arrived(ref, sibsend.at[at], sibrecv.at[at], sibling)

    def weights(stream, phase):
        if phase == 0:
            (load_gu, load_dn)[stream].wait()
            src = (gu32, dn32)[stream]
            rows = ROWS[stream]
            first = pl.multiple_of(dp * rows, 16)
            (wg, wd)[stream][y % 2, pl.ds(first, rows), :] = src[...].astype(jnp.bfloat16)
            if stream == 0:
                pl.semaphore_wait(barrier, len(partners))
            for index in (0, 1, p2(0, 0), p2(0, 1)):
                wstart(stream, index)
            sib(stream, [(0, 0)])
        elif phase == 1:
            for index in (0, 1):
                wwait(stream, index)
            for index in (2, 3, p2(1, 0), p2(1, 1), p2(-1, 0), p2(-1, 1)):
                wstart(stream, index)
        elif phase == 2:
            for index in (p2(0, 0), p2(0, 1)):
                wwait(stream, index)
            for index in (p2(0, 2), p2(0, 3)):
                wstart(stream, index)
            sib(stream, [(1, 0), (-1, 0), (0, 1), (0, -1)])
        elif phase == 3:
            for index in (2, 3):
                wwait(stream, index)
            for index in (p2(2, 0), p2(2, 1)):
                wstart(stream, index)
        elif phase == 4:
            for index in (p2(1, 0), p2(1, 1), p2(-1, 0), p2(-1, 1)):
                wwait(stream, index)
            for index in (p2(1, 2), p2(1, 3), p2(-1, 2), p2(-1, 3)):
                wstart(stream, index)
            sib(stream, [(1, 1), (-1, 1), (1, -1), (-1, -1)])
        elif phase == 5:
            for index in (p2(0, 2), p2(0, 3)):
                wwait(stream, index)
            sib(stream, [(2, 0), (0, 2)])
        elif phase == 6:
            for index in (p2(2, 0), p2(2, 1)):
                wwait(stream, index)
            for index in (p2(2, 2), p2(2, 3)):
                wstart(stream, index)
        elif phase == 7:
            for index in (p2(1, 2), p2(1, 3), p2(-1, 2), p2(-1, 3)):
                wwait(stream, index)
            sib(stream, [(2, 1), (2, -1), (1, 2), (-1, 2)])
        elif phase == 8:
            for index in (p2(2, 2), p2(2, 3)):
                wwait(stream, index)
            sib(stream, [(2, 2)])
            sib_wait(stream)

    def block(source, h):
        return x_buf.at[pl.ds(POS[source] * TOK + h * SUB, SUB), :]

    ag_pending = []

    def ag_start(d, h):
        for way in (0, 1):
            if d == 7 and h != way:
                continue
            src = block((d if way == 0 else NZ - d) % NZ, h)
            dst = block(d + 1 if way == 0 else NZ - d - 1, h)
            at = (way * 8 + d) * 2 + h
            ag_pending.append(
                send(src, dst, agsend.at[at], agrecv.at[at], zr if way == 0 else zl)
            )
            pending.pop()
            if h == 0 and not (d == 7 and way == 1):
                at = way * 8 + d
                send(
                    route.at[(d if way == 0 else NZ - d) % NZ],
                    route.at[d + 1 if way == 0 else NZ - d - 1],
                    rtsend.at[at],
                    rtrecv.at[at],
                    zr if way == 0 else zl,
                )

    def ag_wait(d, h):
        for way in (0, 1):
            if d == 7 and h != way:
                continue
            dst = block(d + 1 if way == 0 else NZ - d - 1, h)
            at = (way * 8 + d) * 2 + h
            arrived(dst, agsend.at[at], agrecv.at[at], zr if way == 0 else zl)
            if h == 0 and not (d == 7 and way == 1):
                at = way * 8 + d
                arrived(
                    route.at[d + 1 if way == 0 else NZ - d - 1],
                    rtsend.at[at],
                    rtrecv.at[at],
                    zr if way == 0 else zl,
                )

    def ag(i):
        d, h = i // 2, i % 2
        ag_wait(d, h)
        if d < 7:
            ag_start(d + 1, h)

    tri_r = lax.broadcasted_iota(jnp.int32, (GTOK, GTOK), 0)
    tri_c = lax.broadcasted_iota(jnp.int32, (GTOK, GTOK), 1)
    lane = lax.broadcasted_iota(jnp.int32, (8, GTOK), 1)

    def dispatch(g):
        tri = ((tri_r < tri_c) & (tri_r // TOK == tri_c // TOK)).astype(jnp.bfloat16)
        parts = [route[s] for s in ORDER[g * GRP : (g + 1) * GRP]]
        parts = jnp.concatenate([part[:, :TOK] for part in parts], axis=1)
        ids, gates = parts[:TOPK], parts[TOPK:]
        marks, shares = [], []
        for e in (0, 1):
            hit = ids == (e * NZ + z).astype(jnp.float32)
            marks.append(jnp.sum(hit.astype(jnp.float32), axis=0, keepdims=True))
            shares.append(jnp.sum(jnp.where(hit, gates, 0.0), axis=0, keepdims=True))
        slot_iota = lax.broadcasted_iota(jnp.int32, (GSLOT, GTOK), 0)
        picks = []
        for e in (0, 1):
            mark = jnp.broadcast_to(marks[e], (8, GTOK))
            earlier = jnp.dot(
                mark.astype(jnp.bfloat16), tri, preferred_element_type=jnp.float32
            )
            slot = jnp.where(
                mark > 0.5, earlier.astype(jnp.int32) + (lane // TOK) * CAP, -1
            )[:1]
            pick = jnp.where(slot_iota == slot, 1.0, 0.0)
            picks.append(pick)
            share = jnp.sum(pick * shares[e], axis=1, keepdims=True)
            wcol[g, pl.ds(e * GSLOT, GSLOT), :] = jnp.broadcast_to(share, (GSLOT, 128))
        pick = jnp.concatenate(picks, axis=0)
        st[g] = pick.T.astype(jnp.bfloat16)
        pick = pick.astype(jnp.bfloat16)
        b, gi = g // 2, g % 2
        for c in range(0, D, 512):
            rows = jnp.dot(
                pick,
                x_buf[pl.ds(g * GTOK, GTOK), pl.ds(c, 512)],
                preferred_element_type=jnp.float32,
            ).astype(jnp.bfloat16)
            for e in (0, 1):
                xs[b, e, pl.ds(gi * GSLOT, GSLOT), pl.ds(c, 512)] = rows[
                    e * GSLOT : (e + 1) * GSLOT
                ]

    def gate_up(b, e, j):
        lhs = xs[b, e]
        cols = pl.ds(j * 256, 256)
        gate = jnp.dot(lhs, wg[e, :, cols], preferred_element_type=jnp.float32)
        up = jnp.dot(
            lhs, wg[e, :, pl.ds(FF + j * 256, 256)], preferred_element_type=jnp.float32
        )
        hid = gate / (1.0 + jnp.exp(-gate)) * up
        act[b, e, :, cols] = hid.astype(jnp.bfloat16)

    def down(b, e, j):
        cols = pl.ds(j * WIDE, WIDE)
        res = jnp.dot(act[b, e], wd[e, :, cols], preferred_element_type=jnp.float32)
        for gi in (0, 1):
            g = b * 2 + gi
            share = wcol[g, pl.ds(e * GSLOT, GSLOT), :]
            share = jnp.concatenate([share] * (WIDE // 128), axis=1)
            outw[g, pl.ds(e * GSLOT, GSLOT), cols] = (
                res[gi * GSLOT : (gi + 1) * GSLOT] * share
            ).astype(jnp.bfloat16)

    def spread(g, j):
        cols = pl.ds(j * WIDE, WIDE)
        ctr[pl.ds(g * GTOK, GTOK), cols] = jnp.dot(
            st[g], outw[g, :, cols], preferred_element_type=jnp.float32
        )

    def cut(ref, source, h):
        return ref.at[pl.ds(POS[source] * TOK, TOK), pl.ds(h * HALF, HALF)]

    def rs_wait(s, way, h):
        buf = (rsr, rsl)[way].at[s - 1, :, pl.ds(h * HALF, HALF)]
        at = (way * 8 + s - 1) * 2 + h
        arrived(buf, rssend.at[at], rsrecv.at[at], zr if way == 0 else zl)
        return buf

    def rs(s, h):
        for way in (0, 1):
            if s == 0 and h != way:
                continue
            source = 8 + s if way == 0 else 8 - s
            total = cut(ctr, source, h)[...]
            if s > 1 or (s == 1 and h == way):
                total = total + rs_wait(s, way, h)[...].astype(jnp.float32)
            blk = cut(x_buf, source, h)
            blk[...] = total.astype(jnp.bfloat16)
            at = (way * 8 + s) * 2 + h
            dst = (rsr, rsl)[way].at[s, :, pl.ds(h * HALF, HALF)]
            send(blk, dst, rssend.at[at], rsrecv.at[at], zr if way == 0 else zl)

    route[0] = routing_ref[...]
    weights(0, 0)

    for p in range(PAGES):
        at = table_ref[0, p]
        keys[pl.ds(p * PAGE, PAGE), :] = k_ref[at]
        values[pl.ds(p * PAGE, PAGE), :] = v_ref[at]
    scale = 1.0 / math.sqrt(HDIM)
    key_at = lax.broadcasted_iota(jnp.int32, (1, COL), 1)
    end = jnp.int32(0)
    ends = []
    for r in range(REQS):
        end = end + length_ref[0, r]
        ends.append(end)
    key_request = sum((key_at >= e).astype(jnp.int32) for e in ends)

    def attend(i, carry):
        first = pl.multiple_of(i * QROWS, QROWS)
        row_at = first + lax.broadcasted_iota(jnp.int32, (QROWS, 1), 0)
        row_request = sum((row_at >= e).astype(jnp.int32) for e in ends)
        scores = (
            lax.dot_general(
                q_ref[pl.ds(first, QROWS), :],
                keys[...],
                (((1,), (1,)), ((), ())),
                preferred_element_type=jnp.float32,
            )
            * scale
        )
        scores = jnp.where(row_request == key_request, scores, -1e30)
        highest = jnp.max(scores, axis=-1, keepdims=True)
        share = jnp.exp(scores - highest)
        totals = jnp.sum(share, axis=-1, keepdims=True)
        probs = (share * (1.0 / totals)).astype(jnp.bfloat16)
        heads_out[pl.ds(first, QROWS), :] = jnp.dot(
            probs, values[...], preferred_element_type=jnp.float32
        ).astype(jnp.bfloat16)
        return carry

    lax.fori_loop(0, COL // QROWS, attend, 0)
    for k in range(1, NDP):
        to = (dp + k) % NDP
        send(
            heads_out.at[pl.ds(pl.multiple_of(to * TOK, TOK), TOK), :],
            heads_in.at[k],
            hsend.at[k],
            hrecv.at[k],
            peers[k - 1],
        )
    heads_in[0] = heads_out[pl.ds(pl.multiple_of(dp * TOK, TOK), TOK), :]
    weights(0, 1)
    for k in range(1, NDP):
        arrived(heads_in.at[k], hsend.at[k], hrecv.at[k], peers[k - 1])
    squares = jnp.zeros((TOK, HDIM), jnp.float32)
    for h in range(NDP):
        cols = pl.ds(h * HDIM, HDIM)
        attn = heads_in[(dp + NDP - h) % NDP].astype(jnp.float32)
        resid = (hidden_ref[:, cols].astype(jnp.float32) + attn).astype(jnp.bfloat16)
        resid_s[:, cols] = resid
        squares = squares + resid.astype(jnp.float32) * resid.astype(jnp.float32)
    factor = lax.rsqrt(jnp.sum(squares, axis=-1, keepdims=True) * (1.0 / D) + epsilon)
    x_buf[pl.ds(POS[0] * TOK, TOK), :] = (
        resid_s[...].astype(jnp.float32) * factor * gain_ref[...]
    ).astype(jnp.bfloat16)

    ag_start(0, 0)
    ag_start(0, 1)
    plan = [
        "w02", "ag0", "w03", "ag1", "ag2", "w10", "ag3", "dispatch3", "ag4", "w04", "ag5", "w05",
        "ag6", "ag7", "dispatch2", "w06", "ag8", "ag9", "w11", "w07", "ag10", "w12", "ag11", "w08",
        "dispatch1", "ag12", "w13", "gate_up100", "gate_up101", "ag13", "gate_up102", "w14",
        "gate_up103", "ag14", "gate_up110", "gate_up111", "ag15", "w15", "dispatch0", "gate_up112",
        "w16", "gate_up113", "gate_up000", "gate_up001", "gate_up002", "w17", "gate_up003",
        "gate_up010", "gate_up011", "gate_up012", "gate_up013", "w18", "agdone", "down000",
        "down010", "down001", "down011", "spread00", "spread01", "rs00", "down002", "down012",
        "down003", "down013", "spread02", "spread03", "rs01", "spread10", "spread11", "rs10",
        "spread12", "spread13", "rs11", "down100", "down110", "rs20", "down101", "down111", "rs21",
        "down102", "down112", "rs30", "down103", "down113", "rs31", "spread20", "spread21", "rs40",
        "spread22", "spread23", "rs41", "spread30", "spread31", "rs50", "spread32", "spread33",
        "rs51", "rs60", "rs61", "rs70", "rs71",
    ]

    def ag_done():
        for copy in ag_pending:
            copy.wait_send()

    run = {
        "ag": ag, "w": weights, "dispatch": dispatch, "gate_up": gate_up, "down": down,
        "spread": spread, "rs": rs, "agdone": ag_done,
    }
    for item in plan:
        name = item.rstrip("0123456789")
        digits = item[len(name) :]
        run[name](*([int(digits)] if name == "ag" else [int(c) for c in digits]))

    for h in (0, 1):
        cols = pl.ds(h * HALF, HALF)
        total = resid_s[:, cols].astype(jnp.float32) + cut(ctr, 0, h)[...]
        for way in (0, 1):
            total = total + rs_wait(8, way, h)[...].astype(jnp.float32)
        out_ref[:, cols] = total.astype(jnp.bfloat16)
    for copy in pending:
        copy.wait_send()


def moe(table, lengths, queries, keys, values, hidden, gain, routing, gate_up, down):
    vmem = pl.BlockSpec(memory_space=pltpu.VMEM)
    smem = pl.BlockSpec(memory_space=pltpu.SMEM)
    hbm = pl.BlockSpec(memory_space=pl.ANY)
    bf, f32 = jnp.bfloat16, jnp.float32
    dma = pltpu.SemaphoreType.DMA
    return pl.pallas_call(
        moe_kernel,
        out_shape=jax.ShapeDtypeStruct((TOK, D), bf),
        in_specs=[smem] * 2 + [vmem] * 6 + [hbm] * 2,
        out_specs=vmem,
        scratch_shapes=[
            pltpu.VMEM((COL, HDIM), bf),
            pltpu.VMEM((COL, HDIM), bf),
            pltpu.VMEM((COL, HDIM), bf),
            pltpu.VMEM((NDP, TOK, HDIM), bf),
            pltpu.VMEM((NZ, 2 * TOPK, 2 * TOK), f32),
            pltpu.VMEM((NZ * TOK, D), bf),
            pltpu.VMEM((2, D, 2 * FF), bf),
            pltpu.VMEM((2, FF, D), bf),
            pltpu.VMEM((ROWS[0], D), f32),
            pltpu.VMEM((ROWS[1], D), f32),
            pltpu.VMEM((2, 2, 2 * GSLOT, D), bf),
            pltpu.VMEM((2, 2, 2 * GSLOT, FF), bf),
            pltpu.VMEM((NGRP, 2 * GSLOT, D), bf),
            pltpu.VMEM((NGRP, 2 * GSLOT, 128), f32),
            pltpu.VMEM((NGRP, GTOK, 2 * GSLOT), bf),
            pltpu.VMEM((NZ * TOK, D), f32),
            pltpu.VMEM((8, TOK, D), bf),
            pltpu.VMEM((8, TOK, D), bf),
            pltpu.VMEM((TOK, D), bf),
            dma((2,)),
            dma((4 * NMSG,)),
            dma((4 * NMSG,)),
            dma((32,)),
            dma((32,)),
            dma((32,)),
            dma((32,)),
            dma((32,)),
            dma((32,)),
            dma((NDP,)),
            dma((NDP,)),
            dma((16,)),
            dma((16,)),
        ],
        compiler_params=pltpu.CompilerParams(
            collective_id=0, has_side_effects=True, vmem_limit_bytes=56 * 1024 * 1024
        ),
    )(table, lengths, queries, keys, values, hidden, gain, routing, gate_up, down)


def local(
    hidden_in,
    queries,
    key_pool,
    value_pool,
    page_table,
    prompt_lengths,
    expert_ids,
    gate_weights,
    norm_gain,
    trainer_gate_up,
    trainer_down,
):
    routing = jnp.concatenate([expert_ids[0].astype(jnp.float32), gate_weights[0]], axis=1)
    routing = jnp.pad(routing.T, ((0, 0), (0, TOK)))
    mixed = moe(
        page_table,
        prompt_lengths,
        queries[0],
        key_pool,
        value_pool,
        hidden_in[0],
        norm_gain[None],
        routing,
        trainer_gate_up[0],
        trainer_down[0],
    )
    return mixed[None]


def solution(mesh):
    placed = (
        P("expert", "dp", None),
        P("expert", None, "dp"),
        P("expert", None, "dp"),
        P("expert", None, "dp"),
        P("expert", None),
        P("expert", None),
        P("expert", "dp", None),
        P("expert", "dp", None),
        P(),
        P("expert", "dp", None),
        P("expert", "dp", None),
    )
    return jax.shard_map(
        local, mesh=mesh, in_specs=placed, out_specs=P("expert", "dp", None), check_vma=False
    )
```

```python
import math

import jax
import jax.numpy as jnp
from jax import lax
from jax.experimental import pallas as pl
from jax.experimental.pallas import tpu as pltpu
from jax.sharding import PartitionSpec as P

MESH = pl.DeviceIdType.MESH
HDIM = 128
TOPK = 8
D = 2048
FF = 1024
NZ = 16
NDP = 16
TOK = 64
SUB = TOK // 2
CAP = 20
GRP = 4
GSLOT = GRP * CAP
GTOK = GRP * TOK
NGRP = NZ // GRP
WIDE = 512
HALF = D // 2
COL = 1024
PAGE = 128
PAGES = COL // PAGE
REQS = 4
QROWS = 256
epsilon = 1e-05

ORDER = (8, 7, 9, 6, 10, 5, 11, 4, 12, 3, 13, 2, 14, 1, 15, 0)
POS = {s: i for i, s in enumerate(ORDER)}

ROWS = (128, 64, 64)
COL0 = (0, 0, D // 2)
COLS = (2 * FF, D // 2, D // 2)
KS = (0, 1, -1, 2)
NMSG = 4 + 4 * len(KS)


def moe_kernel(
    table_ref,
    length_ref,
    q_ref,
    k_ref,
    v_ref,
    hidden_ref,
    gain_ref,
    routing_ref,
    gu_hbm,
    dn_hbm,
    out_ref,
    keys,
    values,
    heads_out,
    heads_in,
    route,
    x_buf,
    wg,
    wd,
    gu32,
    dn32,
    xs,
    act,
    outw,
    wcol,
    st,
    ctr,
    rsr,
    rsl,
    resid_s,
    load_sem,
    wsend,
    wrecv,
    sibsend,
    sibrecv,
    agsend,
    agrecv,
    rssend,
    rsrecv,
    hsend,
    hrecv,
    rtsend,
    rtrecv,
):
    dp = lax.axis_index("dp")
    ex = lax.axis_index("expert")
    x = dp // 4
    y = ((dp // 2) % 2) * 2 + ex // NZ
    core = dp % 2
    z = ex % NZ

    def dev(xx, yy, zz, cc):
        return ((xx * 2 + yy // 2) * 2 + cc, (yy % 2) * NZ + zz)

    def ring4(v, k):
        return (v + 4 + k) % 4

    sibling = dev(x, y, z, 1 - core)
    zr = dev(x, y, (z + 1) % NZ, core)
    zl = dev(x, y, (z + NZ - 1) % NZ, core)
    xy = {
        (0, 1): dev(ring4(x, 1), y, z, core),
        (0, -1): dev(ring4(x, -1), y, z, core),
        (1, 1): dev(x, ring4(y, 1), z, core),
        (1, -1): dev(x, ring4(y, -1), z, core),
    }

    load_gu = pltpu.make_async_copy(gu_hbm, gu32, load_sem.at[0])
    load_dn = pltpu.make_async_copy(dn_hbm, dn32, load_sem.at[1])
    load_gu.start()
    load_dn.start()

    barrier = pltpu.get_barrier_semaphore()
    peers = [((dp + k) % NDP, ex) for k in range(1, NDP)]
    partners = peers + [zr, zl, xy[1, 1], xy[1, -1]]
    for partner in partners:
        pl.semaphore_signal(barrier, inc=1, device_id=partner, device_id_type=MESH)

    pending = []

    def send(src, dst, ssem, rsem, to):
        copy = pltpu.make_async_remote_copy(
            src_ref=src,
            dst_ref=dst,
            send_sem=ssem,
            recv_sem=rsem,
            device_id=to,
            device_id_type=MESH,
        )
        copy.start()
        pending.append(copy)
        return copy

    def arrived(ref, ssem, rsem, to):
        pltpu.make_async_remote_copy(
            src_ref=ref,
            dst_ref=ref,
            send_sem=ssem,
            recv_sem=rsem,
            device_id=to,
            device_id_type=MESH,
        ).wait_recv()

    def shard(stream, dx, dy, off, n):
        sx, sy = ring4(x, -dx), ring4(y, -dy)
        rows = ROWS[stream]
        first = pl.multiple_of(((sx * 2 + sy // 2) * 2 + core) * rows + off, 16)
        buf = wd if stream else wg
        return buf.at[sy % 2, pl.ds(first, n), pl.ds(COL0[stream], COLS[stream])]

    def piece(stream, half, k1, k2, part):
        h = ROWS[stream] // 2
        q = h // 2
        off, n = (half * h, h) if part is None else (half * h + part * q, q)
        dx, dy = (k1, k2) if half == 0 else (k2, k1)
        return shard(stream, dx, dy, off, n)

    def wmsg(stream, half, index):
        at = (stream * 2 + half) * NMSG + index
        return wsend.at[at], wrecv.at[at]

    def decode(index):
        if index < 4:
            return 0, (1, -1)[index % 2], index >= 2, 0
        return 1, (1, -1)[index % 2], (index - 4) % 4 >= 2, KS[(index - 4) // 4]

    def wstart(stream, index):
        ring, sign, forward, k = decode(index)
        for half in (0, 1):
            axis = ring if half == 0 else 1 - ring
            part = (0 if sign == 1 else 1) if forward else None
            step = sign if forward else 0
            k1, k2 = (step, 0) if ring == 0 else (k, step)
            ref = piece(stream, half, k1, k2, part)
            ssem, rsem = wmsg(stream, half, index)
            send(ref, ref, ssem, rsem, xy[axis, sign])

    def wwait(stream, index):
        ring, sign, forward, k = decode(index)
        for half in (0, 1):
            axis = ring if half == 0 else 1 - ring
            part = (0 if sign == 1 else 1) if forward else None
            step = 2 if forward else sign
            k1, k2 = (step, 0) if ring == 0 else (k, step)
            ref = piece(stream, half, k1, k2, part)
            ssem, rsem = wmsg(stream, half, index)
            arrived(ref, ssem, rsem, xy[axis, sign])

    def p2(k, j):
        return 4 + 4 * KS.index(k) + j

    sib_index = {}

    def sib(stream, places):
        for dx, dy in places:
            at = stream * 16 + (dx % 4) * 4 + (dy % 4)
            ref = shard(stream, dx, dy, 0, ROWS[stream])
            send(ref, ref, sibsend.at[at], sibrecv.at[at], sibling)
            sib_index[at] = (stream, dx, dy)

    def sib_wait(stream):
        for at, (s, dx, dy) in sib_index.items():
            if s == stream:
                sx, sy = ring4(x, -dx), ring4(y, -dy)
                rows = ROWS[stream]
                first = pl.multiple_of(((sx * 2 + sy // 2) * 2 + 1 - core) * rows, 16)
                buf = wd if stream else wg
                cols = pl.ds(COL0[stream], COLS[stream])
                ref = buf.at[sy % 2, pl.ds(first, rows), cols]
                arrived(ref, sibsend.at[at], sibrecv.at[at], sibling)

    def weights(stream, phase):
        if phase == 0:
            if stream < 2:
                (load_gu, load_dn)[stream].wait()
            src = (gu32, dn32, dn32)[stream]
            cols = pl.ds(COL0[stream], COLS[stream])
            rows = ROWS[stream]
            first = pl.multiple_of(dp * rows, 16)
            (wg, wd, wd)[stream][y % 2, pl.ds(first, rows), cols] = src[:, cols].astype(
                jnp.bfloat16
            )
            if stream == 0:
                pl.semaphore_wait(barrier, len(partners))
            for index in (0, 1, p2(0, 0), p2(0, 1)):
                wstart(stream, index)
            sib(stream, [(0, 0)])
        elif phase == 1:
            for index in (0, 1):
                wwait(stream, index)
            for index in (2, 3, p2(1, 0), p2(1, 1), p2(-1, 0), p2(-1, 1)):
                wstart(stream, index)
        elif phase == 2:
            for index in (p2(0, 0), p2(0, 1)):
                wwait(stream, index)
            for index in (p2(0, 2), p2(0, 3)):
                wstart(stream, index)
            sib(stream, [(1, 0), (-1, 0), (0, 1), (0, -1)])
        elif phase == 3:
            for index in (2, 3):
                wwait(stream, index)
            for index in (p2(2, 0), p2(2, 1)):
                wstart(stream, index)
        elif phase == 4:
            for index in (p2(1, 0), p2(1, 1), p2(-1, 0), p2(-1, 1)):
                wwait(stream, index)
            for index in (p2(1, 2), p2(1, 3), p2(-1, 2), p2(-1, 3)):
                wstart(stream, index)
            sib(stream, [(1, 1), (-1, 1), (1, -1), (-1, -1)])
        elif phase == 5:
            for index in (p2(0, 2), p2(0, 3)):
                wwait(stream, index)
            sib(stream, [(2, 0), (0, 2)])
        elif phase == 6:
            for index in (p2(2, 0), p2(2, 1)):
                wwait(stream, index)
            for index in (p2(2, 2), p2(2, 3)):
                wstart(stream, index)
        elif phase == 7:
            for index in (p2(1, 2), p2(1, 3), p2(-1, 2), p2(-1, 3)):
                wwait(stream, index)
            sib(stream, [(2, 1), (2, -1), (1, 2), (-1, 2)])
        elif phase == 8:
            for index in (p2(2, 2), p2(2, 3)):
                wwait(stream, index)
            sib(stream, [(2, 2)])
            sib_wait(stream)

    def block(source, h):
        return x_buf.at[pl.ds(POS[source] * TOK + h * SUB, SUB), :]

    ag_pending = []

    def ag_start(d, h):
        for way in (0, 1):
            if d == 7 and h != way:
                continue
            src = block((d if way == 0 else NZ - d) % NZ, h)
            dst = block(d + 1 if way == 0 else NZ - d - 1, h)
            at = (way * 8 + d) * 2 + h
            ag_pending.append(
                send(src, dst, agsend.at[at], agrecv.at[at], zr if way == 0 else zl)
            )
            pending.pop()
            if h == 0 and not (d == 7 and way == 1):
                at = way * 8 + d
                send(
                    route.at[(d if way == 0 else NZ - d) % NZ],
                    route.at[d + 1 if way == 0 else NZ - d - 1],
                    rtsend.at[at],
                    rtrecv.at[at],
                    zr if way == 0 else zl,
                )

    def ag_wait(d, h):
        for way in (0, 1):
            if d == 7 and h != way:
                continue
            dst = block(d + 1 if way == 0 else NZ - d - 1, h)
            at = (way * 8 + d) * 2 + h
            arrived(dst, agsend.at[at], agrecv.at[at], zr if way == 0 else zl)
            if h == 0 and not (d == 7 and way == 1):
                at = way * 8 + d
                arrived(
                    route.at[d + 1 if way == 0 else NZ - d - 1],
                    rtsend.at[at],
                    rtrecv.at[at],
                    zr if way == 0 else zl,
                )

    def ag(i):
        d, h = i // 2, i % 2
        ag_wait(d, h)
        if d < 7:
            ag_start(d + 1, h)

    tri_r = lax.broadcasted_iota(jnp.int32, (GTOK, GTOK), 0)
    tri_c = lax.broadcasted_iota(jnp.int32, (GTOK, GTOK), 1)
    lane = lax.broadcasted_iota(jnp.int32, (8, GTOK), 1)

    def dispatch(g):
        tri = ((tri_r < tri_c) & (tri_r // TOK == tri_c // TOK)).astype(jnp.bfloat16)
        parts = [route[s] for s in ORDER[g * GRP : (g + 1) * GRP]]
        parts = jnp.concatenate([part[:, :TOK] for part in parts], axis=1)
        ids, gates = parts[:TOPK], parts[TOPK:]
        marks, shares = [], []
        for e in (0, 1):
            hit = ids == (e * NZ + z).astype(jnp.float32)
            marks.append(jnp.sum(hit.astype(jnp.float32), axis=0, keepdims=True))
            shares.append(jnp.sum(jnp.where(hit, gates, 0.0), axis=0, keepdims=True))
        slot_iota = lax.broadcasted_iota(jnp.int32, (GSLOT, GTOK), 0)
        picks = []
        for e in (0, 1):
            mark = jnp.broadcast_to(marks[e], (8, GTOK))
            earlier = jnp.dot(
                mark.astype(jnp.bfloat16), tri, preferred_element_type=jnp.float32
            )
            slot = jnp.where(
                mark > 0.5, earlier.astype(jnp.int32) + (lane // TOK) * CAP, -1
            )[:1]
            pick = jnp.where(slot_iota == slot, 1.0, 0.0)
            picks.append(pick)
            share = jnp.sum(pick * shares[e], axis=1, keepdims=True)
            wcol[g, pl.ds(e * GSLOT, GSLOT), :] = jnp.broadcast_to(share, (GSLOT, 128))
        pick = jnp.concatenate(picks, axis=0)
        st[g] = pick.T.astype(jnp.bfloat16)
        pick = pick.astype(jnp.bfloat16)
        for c in range(0, D, 512):
            rows = jnp.dot(
                pick,
                x_buf[pl.ds(g * GTOK, GTOK), pl.ds(c, 512)],
                preferred_element_type=jnp.float32,
            ).astype(jnp.bfloat16)
            for e in (0, 1):
                xs[e, pl.ds(g * GSLOT, GSLOT), pl.ds(c, 512)] = rows[
                    e * GSLOT : (e + 1) * GSLOT
                ]

    def batch_rows(b):
        return pl.ds(GSLOT, (NGRP - 1) * GSLOT) if b else pl.ds(0, GSLOT)

    def gate_up(b, e, j):
        at = batch_rows(b)
        lhs = xs[e, at, :]
        cols = pl.ds(j * 256, 256)
        gate = jnp.dot(lhs, wg[e, :, cols], preferred_element_type=jnp.float32)
        up = jnp.dot(
            lhs, wg[e, :, pl.ds(FF + j * 256, 256)], preferred_element_type=jnp.float32
        )
        hid = gate / (1.0 + jnp.exp(-gate)) * up
        act[e, at, cols] = hid.astype(jnp.bfloat16)

    def down(b, e, j):
        cols = pl.ds(j * WIDE, WIDE)
        res = jnp.dot(
            act[e, batch_rows(b), :], wd[e, :, cols], preferred_element_type=jnp.float32
        )
        for gi in range(NGRP - 1 if b else 1):
            g = b + gi
            share = wcol[g, pl.ds(e * GSLOT, GSLOT), :]
            share = jnp.concatenate([share] * (WIDE // 128), axis=1)
            outw[g, pl.ds(e * GSLOT, GSLOT), cols] = (
                res[gi * GSLOT : (gi + 1) * GSLOT] * share
            ).astype(jnp.bfloat16)

    def spread(g, j):
        cols = pl.ds(j * WIDE, WIDE)
        ctr[pl.ds(g * GTOK, GTOK), cols] = jnp.dot(
            st[g], outw[g, :, cols], preferred_element_type=jnp.float32
        )

    def cut(ref, source, h):
        return ref.at[pl.ds(POS[source] * TOK, TOK), pl.ds(h * HALF, HALF)]

    def rs_wait(s, way, h):
        buf = (rsr, rsl)[way].at[s - 1, :, pl.ds(h * HALF, HALF)]
        at = (way * 8 + s - 1) * 2 + h
        arrived(buf, rssend.at[at], rsrecv.at[at], zr if way == 0 else zl)
        return buf

    def rs(s, h):
        for way in (0, 1):
            if s == 0 and h != way:
                continue
            source = 8 + s if way == 0 else 8 - s
            total = cut(ctr, source, h)[...]
            if s > 1 or (s == 1 and h == way):
                total = total + rs_wait(s, way, h)[...].astype(jnp.float32)
            blk = cut(x_buf, source, h)
            blk[...] = total.astype(jnp.bfloat16)
            at = (way * 8 + s) * 2 + h
            dst = (rsr, rsl)[way].at[s, :, pl.ds(h * HALF, HALF)]
            send(blk, dst, rssend.at[at], rsrecv.at[at], zr if way == 0 else zl)

    route[0] = routing_ref[...]
    weights(0, 0)

    for p in range(PAGES):
        at = table_ref[0, p]
        keys[pl.ds(p * PAGE, PAGE), :] = k_ref[at]
        values[pl.ds(p * PAGE, PAGE), :] = v_ref[at]
    scale = 1.0 / math.sqrt(HDIM)
    key_at = lax.broadcasted_iota(jnp.int32, (1, COL), 1)
    end = jnp.int32(0)
    ends = []
    for r in range(REQS):
        end = end + length_ref[0, r]
        ends.append(end)
    key_request = sum((key_at >= e).astype(jnp.int32) for e in ends)

    def attend(i, carry):
        first = pl.multiple_of(i * QROWS, QROWS)
        row_at = first + lax.broadcasted_iota(jnp.int32, (QROWS, 1), 0)
        row_request = sum((row_at >= e).astype(jnp.int32) for e in ends)
        scores = (
            lax.dot_general(
                q_ref[pl.ds(first, QROWS), :],
                keys[...],
                (((1,), (1,)), ((), ())),
                preferred_element_type=jnp.float32,
            )
            * scale
        )
        scores = jnp.where(row_request == key_request, scores, -1e30)
        highest = jnp.max(scores, axis=-1, keepdims=True)
        share = jnp.exp(scores - highest)
        totals = jnp.sum(share, axis=-1, keepdims=True)
        probs = (share * (1.0 / totals)).astype(jnp.bfloat16)
        heads_out[pl.ds(first, QROWS), :] = jnp.dot(
            probs, values[...], preferred_element_type=jnp.float32
        ).astype(jnp.bfloat16)
        return carry

    lax.fori_loop(0, COL // QROWS, attend, 0)
    for k in range(1, NDP):
        to = (dp + k) % NDP
        send(
            heads_out.at[pl.ds(pl.multiple_of(to * TOK, TOK), TOK), :],
            heads_in.at[k],
            hsend.at[k],
            hrecv.at[k],
            peers[k - 1],
        )
    heads_in[0] = heads_out[pl.ds(pl.multiple_of(dp * TOK, TOK), TOK), :]
    weights(0, 1)
    for k in range(1, NDP):
        arrived(heads_in.at[k], hsend.at[k], hrecv.at[k], peers[k - 1])
    squares = jnp.zeros((TOK, HDIM), jnp.float32)
    for h in range(NDP):
        cols = pl.ds(h * HDIM, HDIM)
        attn = heads_in[(dp + NDP - h) % NDP].astype(jnp.float32)
        resid = (hidden_ref[:, cols].astype(jnp.float32) + attn).astype(jnp.bfloat16)
        resid_s[:, cols] = resid
        squares = squares + resid.astype(jnp.float32) * resid.astype(jnp.float32)
    factor = lax.rsqrt(jnp.sum(squares, axis=-1, keepdims=True) * (1.0 / D) + epsilon)
    x_buf[pl.ds(POS[0] * TOK, TOK), :] = (
        resid_s[...].astype(jnp.float32) * factor * gain_ref[...]
    ).astype(jnp.bfloat16)

    ag_start(0, 0)
    ag_start(0, 1)
    plan = [
        "w02", "ag0", "w03", "ag1", "ag2", "w10", "ag3", "dispatch3", "ag4", "w04", "ag5", "w05",
        "ag6", "ag7", "dispatch2", "w06", "ag8", "w11", "ag9", "w20", "w07", "ag10", "w12", "ag11",
        "w08", "dispatch1", "w13", "gate_up100", "ag12", "w14", "gate_up101", "w21", "gate_up102",
        "ag13", "w22", "gate_up103", "w15", "gate_up110", "ag14", "w16", "gate_up111", "w23",
        "gate_up112", "w17", "gate_up113", "ag15", "w24", "dispatch0", "gate_up000", "w18",
        "gate_up001", "gate_up002", "w25", "gate_up003", "gate_up010", "w26", "gate_up011",
        "gate_up012", "gate_up013", "agdone", "down000", "down010", "down001", "down011",
        "spread00", "spread01", "rs00", "w27", "down100", "down110", "rs10", "down101", "down111",
        "spread10", "spread11", "w28", "down002", "down012", "down003", "down013", "spread02",
        "spread03", "rs01", "rs20", "down102", "down112", "rs11", "rs30", "down103", "down113",
        "spread12", "spread13", "rs21", "spread20", "spread21", "rs40", "rs31", "spread22",
        "spread23", "spread30", "spread31", "rs50", "rs41", "rs60", "spread32", "spread33", "rs51",
        "rs70", "rs61", "rs71",
    ]

    def ag_done():
        for copy in ag_pending:
            copy.wait_send()

    run = {
        "ag": ag, "w": weights, "dispatch": dispatch, "gate_up": gate_up, "down": down,
        "spread": spread, "rs": rs, "agdone": ag_done,
    }
    for item in plan:
        name = item.rstrip("0123456789")
        digits = item[len(name) :]
        run[name](*([int(digits)] if name == "ag" else [int(c) for c in digits]))

    for h in (0, 1):
        cols = pl.ds(h * HALF, HALF)
        total = resid_s[:, cols].astype(jnp.float32) + cut(ctr, 0, h)[...]
        for way in (0, 1):
            total = total + rs_wait(8, way, h)[...].astype(jnp.float32)
        out_ref[:, cols] = total.astype(jnp.bfloat16)
    for copy in pending:
        copy.wait_send()


def moe(table, lengths, queries, keys, values, hidden, gain, routing, gate_up, down):
    vmem = pl.BlockSpec(memory_space=pltpu.VMEM)
    smem = pl.BlockSpec(memory_space=pltpu.SMEM)
    hbm = pl.BlockSpec(memory_space=pl.ANY)
    bf, f32 = jnp.bfloat16, jnp.float32
    dma = pltpu.SemaphoreType.DMA
    return pl.pallas_call(
        moe_kernel,
        out_shape=jax.ShapeDtypeStruct((TOK, D), bf),
        in_specs=[smem] * 2 + [vmem] * 6 + [hbm] * 2,
        out_specs=vmem,
        scratch_shapes=[
            pltpu.VMEM((COL, HDIM), bf),
            pltpu.VMEM((COL, HDIM), bf),
            pltpu.VMEM((COL, HDIM), bf),
            pltpu.VMEM((NDP, TOK, HDIM), bf),
            pltpu.VMEM((NZ, 2 * TOPK, 2 * TOK), f32),
            pltpu.VMEM((NZ * TOK, D), bf),
            pltpu.VMEM((2, D, 2 * FF), bf),
            pltpu.VMEM((2, FF, D), bf),
            pltpu.VMEM((ROWS[0], D), f32),
            pltpu.VMEM((ROWS[1], D), f32),
            pltpu.VMEM((2, NGRP * GSLOT, D), bf),
            pltpu.VMEM((2, NGRP * GSLOT, FF), bf),
            pltpu.VMEM((NGRP, 2 * GSLOT, D), bf),
            pltpu.VMEM((NGRP, 2 * GSLOT, 128), f32),
            pltpu.VMEM((NGRP, GTOK, 2 * GSLOT), bf),
            pltpu.VMEM((NZ * TOK, D), f32),
            pltpu.VMEM((8, TOK, D), bf),
            pltpu.VMEM((8, TOK, D), bf),
            pltpu.VMEM((TOK, D), bf),
            dma((2,)),
            dma((6 * NMSG,)),
            dma((6 * NMSG,)),
            dma((48,)),
            dma((48,)),
            dma((32,)),
            dma((32,)),
            dma((32,)),
            dma((32,)),
            dma((NDP,)),
            dma((NDP,)),
            dma((16,)),
            dma((16,)),
        ],
        compiler_params=pltpu.CompilerParams(
            collective_id=0, has_side_effects=True, vmem_limit_bytes=56 * 1024 * 1024
        ),
    )(table, lengths, queries, keys, values, hidden, gain, routing, gate_up, down)


def local(
    hidden_in,
    queries,
    key_pool,
    value_pool,
    page_table,
    prompt_lengths,
    expert_ids,
    gate_weights,
    norm_gain,
    trainer_gate_up,
    trainer_down,
):
    routing = jnp.concatenate([expert_ids[0].astype(jnp.float32), gate_weights[0]], axis=1)
    routing = jnp.pad(routing.T, ((0, 0), (0, TOK)))
    mixed = moe(
        page_table,
        prompt_lengths,
        queries[0],
        key_pool,
        value_pool,
        hidden_in[0],
        norm_gain[None],
        routing,
        trainer_gate_up[0],
        trainer_down[0],
    )
    return mixed[None]


def solution(mesh):
    placed = (
        P("expert", "dp", None),
        P("expert", None, "dp"),
        P("expert", None, "dp"),
        P("expert", None, "dp"),
        P("expert", None),
        P("expert", None),
        P("expert", "dp", None),
        P("expert", "dp", None),
        P(),
        P("expert", "dp", None),
        P("expert", "dp", None),
    )
    return jax.shard_map(
        local, mesh=mesh, in_specs=placed, out_specs=P("expert", "dp", None), check_vma=False
    )
```

```python
import math

import jax
import jax.numpy as jnp
from jax import lax
from jax.experimental import pallas as pl
from jax.experimental.pallas import tpu as pltpu
from jax.sharding import PartitionSpec as P

MESH = pl.DeviceIdType.MESH
HDIM = 128
TOPK = 8
D = 2048
FF = 1024
NZ = 16
NDP = 16
TOK = 64
SUB = TOK // 2
CAP = 20
GRP = 4
GSLOT = GRP * CAP
GTOK = GRP * TOK
NGRP = NZ // GRP
WIDE = 512
HALF = D // 2
COL = 1024
PAGE = 128
PAGES = COL // PAGE
REQS = 4
QROWS = 256
epsilon = 1e-05

ORDER = (8, 7, 9, 6, 10, 5, 11, 4, 12, 3, 13, 2, 14, 1, 15, 0)
POS = {s: i for i, s in enumerate(ORDER)}

ROWS = (128, 64)
KS = (0, 1, -1, 2)
NMSG = 4 + 4 * len(KS)


def moe_kernel(
    table_ref,
    length_ref,
    q_hbm,
    k_hbm,
    v_hbm,
    hidden_hbm,
    gain_ref,
    ids_ref,
    gates_ref,
    gu_hbm,
    dn_hbm,
    out_ref,
    q_ref,
    k_ref,
    v_ref,
    hidden_ref,
    keys,
    values,
    heads_out,
    heads_in,
    route,
    x_buf,
    wg,
    wd,
    gu32,
    dn32,
    xs,
    act,
    outw,
    wcol,
    st,
    ctr,
    rsr,
    rsl,
    resid_s,
    load_sem,
    wsend,
    wrecv,
    sibsend,
    sibrecv,
    agsend,
    agrecv,
    rssend,
    rsrecv,
    hsend,
    hrecv,
    rtsend,
    rtrecv,
):
    dp = lax.axis_index("dp")
    ex = lax.axis_index("expert")
    x = dp // 4
    y = ((dp // 2) % 2) * 2 + ex // NZ
    core = dp % 2
    z = ex % NZ

    def dev(xx, yy, zz, cc):
        return ((xx * 2 + yy // 2) * 2 + cc, (yy % 2) * NZ + zz)

    def ring4(v, k):
        return (v + 4 + k) % 4

    sibling = dev(x, y, z, 1 - core)
    zr = dev(x, y, (z + 1) % NZ, core)
    zl = dev(x, y, (z + NZ - 1) % NZ, core)
    xy = {
        (0, 1): dev(ring4(x, 1), y, z, core),
        (0, -1): dev(ring4(x, -1), y, z, core),
        (1, 1): dev(x, ring4(y, 1), z, core),
        (1, -1): dev(x, ring4(y, -1), z, core),
    }

    load_gu = pltpu.make_async_copy(gu_hbm, gu32, load_sem.at[0])
    load_dn = pltpu.make_async_copy(dn_hbm, dn32, load_sem.at[1])
    inputs = [
        pltpu.make_async_copy(src, dst, load_sem.at[2 + i])
        for i, (src, dst) in enumerate(
            [(k_hbm, k_ref), (v_hbm, v_ref), (q_hbm, q_ref), (hidden_hbm, hidden_ref)]
        )
    ]
    load_gu.start()
    for copy in inputs:
        copy.start()
    load_dn.start()

    barrier = pltpu.get_barrier_semaphore()
    peers = [((dp + k) % NDP, ex) for k in range(1, NDP)]
    partners = peers + [zr, zl, xy[1, 1], xy[1, -1]]
    for partner in partners:
        pl.semaphore_signal(barrier, inc=1, device_id=partner, device_id_type=MESH)

    pending = []

    def send(src, dst, ssem, rsem, to):
        copy = pltpu.make_async_remote_copy(
            src_ref=src,
            dst_ref=dst,
            send_sem=ssem,
            recv_sem=rsem,
            device_id=to,
            device_id_type=MESH,
        )
        copy.start()
        pending.append(copy)
        return copy

    def arrived(ref, ssem, rsem, to):
        pltpu.make_async_remote_copy(
            src_ref=ref,
            dst_ref=ref,
            send_sem=ssem,
            recv_sem=rsem,
            device_id=to,
            device_id_type=MESH,
        ).wait_recv()

    def shard(stream, dx, dy, off, n):
        sx, sy = ring4(x, -dx), ring4(y, -dy)
        rows = ROWS[stream]
        first = pl.multiple_of(((sx * 2 + sy // 2) * 2 + core) * rows + off, 16)
        buf = wd if stream else wg
        return buf.at[sy % 2, pl.ds(first, n), :]

    def piece(stream, half, k1, k2, part):
        h = ROWS[stream] // 2
        q = h // 2
        off, n = (half * h, h) if part is None else (half * h + part * q, q)
        dx, dy = (k1, k2) if half == 0 else (k2, k1)
        return shard(stream, dx, dy, off, n)

    def wmsg(stream, half, index):
        at = (stream * 2 + half) * NMSG + index
        return wsend.at[at], wrecv.at[at]

    def decode(index):
        if index < 4:
            return 0, (1, -1)[index % 2], index >= 2, 0
        return 1, (1, -1)[index % 2], (index - 4) % 4 >= 2, KS[(index - 4) // 4]

    def wstart(stream, index):
        ring, sign, forward, k = decode(index)
        for half in (0, 1):
            axis = ring if half == 0 else 1 - ring
            part = (0 if sign == 1 else 1) if forward else None
            step = sign if forward else 0
            k1, k2 = (step, 0) if ring == 0 else (k, step)
            ref = piece(stream, half, k1, k2, part)
            ssem, rsem = wmsg(stream, half, index)
            send(ref, ref, ssem, rsem, xy[axis, sign])

    def wwait(stream, index):
        ring, sign, forward, k = decode(index)
        for half in (0, 1):
            axis = ring if half == 0 else 1 - ring
            part = (0 if sign == 1 else 1) if forward else None
            step = 2 if forward else sign
            k1, k2 = (step, 0) if ring == 0 else (k, step)
            ref = piece(stream, half, k1, k2, part)
            ssem, rsem = wmsg(stream, half, index)
            arrived(ref, ssem, rsem, xy[axis, sign])

    def p2(k, j):
        return 4 + 4 * KS.index(k) + j

    sib_index = {}

    def sib(stream, places):
        for dx, dy in places:
            at = stream * 16 + (dx % 4) * 4 + (dy % 4)
            ref = shard(stream, dx, dy, 0, ROWS[stream])
            send(ref, ref, sibsend.at[at], sibrecv.at[at], sibling)
            sib_index[at] = (stream, dx, dy)

    def sib_wait(stream):
        for at, (s, dx, dy) in sib_index.items():
            if s == stream:
                sx, sy = ring4(x, -dx), ring4(y, -dy)
                rows = ROWS[stream]
                first = pl.multiple_of(((sx * 2 + sy // 2) * 2 + 1 - core) * rows, 16)
                buf = wd if stream else wg
                ref = buf.at[sy % 2, pl.ds(first, rows), :]
                arrived(ref, sibsend.at[at], sibrecv.at[at], sibling)

    def weights(stream, phase):
        if phase == 0:
            (load_gu, load_dn)[stream].wait()
            src = (gu32, dn32)[stream]
            rows = ROWS[stream]
            first = pl.multiple_of(dp * rows, 16)
            (wg, wd)[stream][y % 2, pl.ds(first, rows), :] = src[...].astype(jnp.bfloat16)
            if stream == 0:
                pl.semaphore_wait(barrier, len(partners))
            for index in (0, 1, p2(0, 0), p2(0, 1)):
                wstart(stream, index)
            sib(stream, [(0, 0)])
        elif phase == 1:
            for index in (0, 1):
                wwait(stream, index)
            for index in (2, 3, p2(1, 0), p2(1, 1), p2(-1, 0), p2(-1, 1)):
                wstart(stream, index)
        elif phase == 2:
            for index in (p2(0, 0), p2(0, 1)):
                wwait(stream, index)
            for index in (p2(0, 2), p2(0, 3)):
                wstart(stream, index)
            sib(stream, [(1, 0), (-1, 0), (0, 1), (0, -1)])
        elif phase == 3:
            for index in (2, 3):
                wwait(stream, index)
            for index in (p2(2, 0), p2(2, 1)):
                wstart(stream, index)
        elif phase == 4:
            for index in (p2(1, 0), p2(1, 1), p2(-1, 0), p2(-1, 1)):
                wwait(stream, index)
            for index in (p2(1, 2), p2(1, 3), p2(-1, 2), p2(-1, 3)):
                wstart(stream, index)
            sib(stream, [(1, 1), (-1, 1), (1, -1), (-1, -1)])
        elif phase == 5:
            for index in (p2(0, 2), p2(0, 3)):
                wwait(stream, index)
            sib(stream, [(2, 0), (0, 2)])
        elif phase == 6:
            for index in (p2(2, 0), p2(2, 1)):
                wwait(stream, index)
            for index in (p2(2, 2), p2(2, 3)):
                wstart(stream, index)
        elif phase == 7:
            for index in (p2(1, 2), p2(1, 3), p2(-1, 2), p2(-1, 3)):
                wwait(stream, index)
            sib(stream, [(2, 1), (2, -1), (1, 2), (-1, 2)])
        elif phase == 8:
            for index in (p2(2, 2), p2(2, 3)):
                wwait(stream, index)
            sib(stream, [(2, 2)])
            sib_wait(stream)

    def block(source, h):
        return x_buf.at[pl.ds(POS[source] * TOK + h * SUB, SUB), :]

    ag_pending = []

    def ag_start(d, h):
        for way in (0, 1):
            if d == 7 and h != way:
                continue
            src = block((d if way == 0 else NZ - d) % NZ, h)
            dst = block(d + 1 if way == 0 else NZ - d - 1, h)
            at = (way * 8 + d) * 2 + h
            ag_pending.append(
                send(src, dst, agsend.at[at], agrecv.at[at], zr if way == 0 else zl)
            )
            pending.pop()
            if h == 0 and not (d == 7 and way == 1):
                at = way * 8 + d
                send(
                    route.at[(d if way == 0 else NZ - d) % NZ],
                    route.at[d + 1 if way == 0 else NZ - d - 1],
                    rtsend.at[at],
                    rtrecv.at[at],
                    zr if way == 0 else zl,
                )

    def ag_wait(d, h):
        for way in (0, 1):
            if d == 7 and h != way:
                continue
            dst = block(d + 1 if way == 0 else NZ - d - 1, h)
            at = (way * 8 + d) * 2 + h
            arrived(dst, agsend.at[at], agrecv.at[at], zr if way == 0 else zl)
            if h == 0 and not (d == 7 and way == 1):
                at = way * 8 + d
                arrived(
                    route.at[d + 1 if way == 0 else NZ - d - 1],
                    rtsend.at[at],
                    rtrecv.at[at],
                    zr if way == 0 else zl,
                )

    def ag(i):
        d, h = i // 2, i % 2
        ag_wait(d, h)
        if d < 7:
            ag_start(d + 1, h)

    tri_r = lax.broadcasted_iota(jnp.int32, (GTOK, GTOK), 0)
    tri_c = lax.broadcasted_iota(jnp.int32, (GTOK, GTOK), 1)
    lane = lax.broadcasted_iota(jnp.int32, (8, GTOK), 1)

    def dispatch(g):
        tri = ((tri_r < tri_c) & (tri_r // TOK == tri_c // TOK)).astype(jnp.bfloat16)
        parts = [route[s] for s in ORDER[g * GRP : (g + 1) * GRP]]
        parts = jnp.concatenate([part[:, :TOK] for part in parts], axis=1)
        ids, gates = parts[:TOPK], parts[TOPK:]
        marks, shares = [], []
        for e in (0, 1):
            hit = ids == (e * NZ + z).astype(jnp.float32)
            marks.append(jnp.sum(hit.astype(jnp.float32), axis=0, keepdims=True))
            shares.append(jnp.sum(jnp.where(hit, gates, 0.0), axis=0, keepdims=True))
        slot_iota = lax.broadcasted_iota(jnp.int32, (GSLOT, GTOK), 0)
        picks = []
        for e in (0, 1):
            mark = jnp.broadcast_to(marks[e], (8, GTOK))
            earlier = jnp.dot(
                mark.astype(jnp.bfloat16), tri, preferred_element_type=jnp.float32
            )
            slot = jnp.where(
                mark > 0.5, earlier.astype(jnp.int32) + (lane // TOK) * CAP, -1
            )[:1]
            pick = jnp.where(slot_iota == slot, 1.0, 0.0)
            picks.append(pick)
            share = jnp.sum(pick * shares[e], axis=1, keepdims=True)
            wcol[g, pl.ds(e * GSLOT, GSLOT), :] = jnp.broadcast_to(share, (GSLOT, 128))
        pick = jnp.concatenate(picks, axis=0)
        st[g] = pick.T.astype(jnp.bfloat16)
        pick = pick.astype(jnp.bfloat16)
        b, gi = g // 2, g % 2
        for c in range(0, D, 512):
            rows = jnp.dot(
                pick,
                x_buf[pl.ds(g * GTOK, GTOK), pl.ds(c, 512)],
                preferred_element_type=jnp.float32,
            ).astype(jnp.bfloat16)
            for e in (0, 1):
                xs[b, e, pl.ds(gi * GSLOT, GSLOT), pl.ds(c, 512)] = rows[
                    e * GSLOT : (e + 1) * GSLOT
                ]

    def gate_up(b, e, j):
        lhs = xs[b, e]
        cols = pl.ds(j * 256, 256)
        gate = jnp.dot(lhs, wg[e, :, cols], preferred_element_type=jnp.float32)
        up = jnp.dot(
            lhs, wg[e, :, pl.ds(FF + j * 256, 256)], preferred_element_type=jnp.float32
        )
        hid = gate / (1.0 + jnp.exp(-gate)) * up
        act[b, e, :, cols] = hid.astype(jnp.bfloat16)

    def down(b, e, j):
        cols = pl.ds(j * WIDE, WIDE)
        res = jnp.dot(act[b, e], wd[e, :, cols], preferred_element_type=jnp.float32)
        for gi in (0, 1):
            g = b * 2 + gi
            share = wcol[g, pl.ds(e * GSLOT, GSLOT), :]
            share = jnp.concatenate([share] * (WIDE // 128), axis=1)
            outw[g, pl.ds(e * GSLOT, GSLOT), cols] = (
                res[gi * GSLOT : (gi + 1) * GSLOT] * share
            ).astype(jnp.bfloat16)

    def spread(g, j):
        cols = pl.ds(j * WIDE, WIDE)
        ctr[pl.ds(g * GTOK, GTOK), cols] = jnp.dot(
            st[g], outw[g, :, cols], preferred_element_type=jnp.float32
        )

    def cut(ref, source, h):
        return ref.at[pl.ds(POS[source] * TOK, TOK), pl.ds(h * HALF, HALF)]

    def rs_wait(s, way, h):
        buf = (rsr, rsl)[way].at[s - 1, :, pl.ds(h * HALF, HALF)]
        at = (way * 8 + s - 1) * 2 + h
        arrived(buf, rssend.at[at], rsrecv.at[at], zr if way == 0 else zl)
        return buf

    def rs(s, h):
        for way in (0, 1):
            if s == 0 and h != way:
                continue
            source = 8 + s if way == 0 else 8 - s
            total = cut(ctr, source, h)[...]
            if s > 1 or (s == 1 and h == way):
                total = total + rs_wait(s, way, h)[...].astype(jnp.float32)
            blk = cut(x_buf, source, h)
            blk[...] = total.astype(jnp.bfloat16)
            at = (way * 8 + s) * 2 + h
            dst = (rsr, rsl)[way].at[s, :, pl.ds(h * HALF, HALF)]
            send(blk, dst, rssend.at[at], rsrecv.at[at], zr if way == 0 else zl)

    route[0] = jnp.zeros((2 * TOPK, 2 * TOK), jnp.float32)
    route[0, pl.ds(0, TOPK), pl.ds(0, TOK)] = ids_ref[...].astype(jnp.float32)
    route[0, pl.ds(TOPK, TOPK), pl.ds(0, TOK)] = gates_ref[...]
    weights(0, 0)

    for copy in inputs:
        copy.wait()
    for p in range(PAGES):
        at = table_ref[0, p]
        keys[pl.ds(p * PAGE, PAGE), :] = k_ref[at]
        values[pl.ds(p * PAGE, PAGE), :] = v_ref[at]
    scale = 1.0 / math.sqrt(HDIM)
    key_at = lax.broadcasted_iota(jnp.int32, (1, COL), 1)
    end = jnp.int32(0)
    ends = []
    for r in range(REQS):
        end = end + length_ref[0, r]
        ends.append(end)
    key_request = sum((key_at >= e).astype(jnp.int32) for e in ends)

    def attend(i, carry):
        first = pl.multiple_of(i * QROWS, QROWS)
        row_at = first + lax.broadcasted_iota(jnp.int32, (QROWS, 1), 0)
        row_request = sum((row_at >= e).astype(jnp.int32) for e in ends)
        scores = (
            lax.dot_general(
                q_ref[pl.ds(first, QROWS), :],
                keys[...],
                (((1,), (1,)), ((), ())),
                preferred_element_type=jnp.float32,
            )
            * scale
        )
        scores = jnp.where(row_request == key_request, scores, -1e30)
        highest = jnp.max(scores, axis=-1, keepdims=True)
        share = jnp.exp(scores - highest)
        totals = jnp.sum(share, axis=-1, keepdims=True)
        probs = (share * (1.0 / totals)).astype(jnp.bfloat16)
        heads_out[pl.ds(first, QROWS), :] = jnp.dot(
            probs, values[...], preferred_element_type=jnp.float32
        ).astype(jnp.bfloat16)
        return carry

    lax.fori_loop(0, COL // QROWS, attend, 0)
    for k in range(1, NDP):
        to = (dp + k) % NDP
        send(
            heads_out.at[pl.ds(pl.multiple_of(to * TOK, TOK), TOK), :],
            heads_in.at[k],
            hsend.at[k],
            hrecv.at[k],
            peers[k - 1],
        )
    heads_in[0] = heads_out[pl.ds(pl.multiple_of(dp * TOK, TOK), TOK), :]
    weights(0, 1)
    for k in range(1, NDP):
        arrived(heads_in.at[k], hsend.at[k], hrecv.at[k], peers[k - 1])
    squares = jnp.zeros((TOK, HDIM), jnp.float32)
    for h in range(NDP):
        cols = pl.ds(h * HDIM, HDIM)
        attn = heads_in[(dp + NDP - h) % NDP].astype(jnp.float32)
        resid = (hidden_ref[:, cols].astype(jnp.float32) + attn).astype(jnp.bfloat16)
        resid_s[:, cols] = resid
        squares = squares + resid.astype(jnp.float32) * resid.astype(jnp.float32)
    factor = lax.rsqrt(jnp.sum(squares, axis=-1, keepdims=True) * (1.0 / D) + epsilon)
    x_buf[pl.ds(POS[0] * TOK, TOK), :] = (
        resid_s[...].astype(jnp.float32) * factor * gain_ref[...]
    ).astype(jnp.bfloat16)

    ag_start(0, 0)
    ag_start(0, 1)
    plan = [
        "w02", "ag0", "w03", "ag1", "ag2", "w10", "ag3", "dispatch3", "ag4", "w04", "ag5", "w05",
        "ag6", "ag7", "dispatch2", "w06", "ag8", "ag9", "w11", "w07", "ag10", "w12", "ag11", "w08",
        "dispatch1", "ag12", "w13", "gate_up100", "gate_up101", "ag13", "gate_up102", "w14",
        "gate_up103", "ag14", "gate_up110", "gate_up111", "ag15", "w15", "dispatch0", "gate_up112",
        "w16", "gate_up113", "gate_up000", "gate_up001", "gate_up002", "w17", "gate_up003",
        "gate_up010", "gate_up011", "gate_up012", "gate_up013", "w18", "agdone", "down000",
        "down010", "down001", "down011", "spread00", "spread01", "rs00", "down002", "down012",
        "down003", "down013", "spread02", "spread03", "rs01", "spread10", "spread11", "rs10",
        "spread12", "spread13", "rs11", "down100", "down110", "rs20", "down101", "down111", "rs21",
        "down102", "down112", "rs30", "down103", "down113", "rs31", "spread20", "spread21", "rs40",
        "spread22", "spread23", "rs41", "spread30", "spread31", "rs50", "spread32", "spread33",
        "rs51", "rs60", "rs61", "rs70", "rs71",
    ]

    def ag_done():
        for copy in ag_pending:
            copy.wait_send()

    run = {
        "ag": ag, "w": weights, "dispatch": dispatch, "gate_up": gate_up, "down": down,
        "spread": spread, "rs": rs, "agdone": ag_done,
    }
    for item in plan:
        name = item.rstrip("0123456789")
        digits = item[len(name) :]
        run[name](*([int(digits)] if name == "ag" else [int(c) for c in digits]))

    for h in (0, 1):
        cols = pl.ds(h * HALF, HALF)
        total = resid_s[:, cols].astype(jnp.float32) + cut(ctr, 0, h)[...]
        for way in (0, 1):
            total = total + rs_wait(8, way, h)[...].astype(jnp.float32)
        out_ref[:, cols] = total.astype(jnp.bfloat16)
    for copy in pending:
        copy.wait_send()


def moe(table, lengths, queries, keys, values, hidden, gain, ids, gates, gate_up, down):
    vmem = pl.BlockSpec(memory_space=pltpu.VMEM)
    smem = pl.BlockSpec(memory_space=pltpu.SMEM)
    hbm = pl.BlockSpec(memory_space=pl.ANY)
    bf, f32 = jnp.bfloat16, jnp.float32
    dma = pltpu.SemaphoreType.DMA
    return pl.pallas_call(
        moe_kernel,
        out_shape=jax.ShapeDtypeStruct((TOK, D), bf),
        in_specs=[smem] * 2 + [hbm] * 4 + [vmem] * 3 + [hbm] * 2,
        out_specs=vmem,
        scratch_shapes=[
            pltpu.VMEM((COL, HDIM), bf),
            pltpu.VMEM((PAGES, PAGE, HDIM), bf),
            pltpu.VMEM((PAGES, PAGE, HDIM), bf),
            pltpu.VMEM((TOK, D), bf),
            pltpu.VMEM((COL, HDIM), bf),
            pltpu.VMEM((COL, HDIM), bf),
            pltpu.VMEM((COL, HDIM), bf),
            pltpu.VMEM((NDP, TOK, HDIM), bf),
            pltpu.VMEM((NZ, 2 * TOPK, 2 * TOK), f32),
            pltpu.VMEM((NZ * TOK, D), bf),
            pltpu.VMEM((2, D, 2 * FF), bf),
            pltpu.VMEM((2, FF, D), bf),
            pltpu.VMEM((ROWS[0], D), f32),
            pltpu.VMEM((ROWS[1], D), f32),
            pltpu.VMEM((2, 2, 2 * GSLOT, D), bf),
            pltpu.VMEM((2, 2, 2 * GSLOT, FF), bf),
            pltpu.VMEM((NGRP, 2 * GSLOT, D), bf),
            pltpu.VMEM((NGRP, 2 * GSLOT, 128), f32),
            pltpu.VMEM((NGRP, GTOK, 2 * GSLOT), bf),
            pltpu.VMEM((NZ * TOK, D), f32),
            pltpu.VMEM((8, TOK, D), bf),
            pltpu.VMEM((8, TOK, D), bf),
            pltpu.VMEM((TOK, D), bf),
            dma((6,)),
            dma((4 * NMSG,)),
            dma((4 * NMSG,)),
            dma((32,)),
            dma((32,)),
            dma((32,)),
            dma((32,)),
            dma((32,)),
            dma((32,)),
            dma((NDP,)),
            dma((NDP,)),
            dma((16,)),
            dma((16,)),
        ],
        compiler_params=pltpu.CompilerParams(
            collective_id=0, has_side_effects=True, vmem_limit_bytes=56 * 1024 * 1024
        ),
    )(table, lengths, queries, keys, values, hidden, gain, ids, gates, gate_up, down)


def local(
    hidden_in,
    queries,
    key_pool,
    value_pool,
    page_table,
    prompt_lengths,
    expert_ids,
    gate_weights,
    norm_gain,
    trainer_gate_up,
    trainer_down,
):
    mixed = moe(
        page_table,
        prompt_lengths,
        queries[0],
        key_pool,
        value_pool,
        hidden_in[0],
        norm_gain[None],
        expert_ids[0].T,
        gate_weights[0].T,
        trainer_gate_up[0],
        trainer_down[0],
    )
    return mixed[None]


def solution(mesh):
    placed = (
        P("expert", "dp", None),
        P("expert", None, "dp"),
        P("expert", None, "dp"),
        P("expert", None, "dp"),
        P("expert", None),
        P("expert", None),
        P("expert", "dp", None),
        P("expert", "dp", None),
        P(),
        P("expert", "dp", None),
        P("expert", "dp", None),
    )
    return jax.shard_map(
        local, mesh=mesh, in_specs=placed, out_specs=P("expert", "dp", None), check_vma=False
    )
```
